32 devices in a mesh: dp: 8 (over z, x), grp: 4 (over y, core).
Axes of the slice: x: 2, y: 2, z: 4, core: 2. Of those that a mesh axis runs over, the one named last changes fastest.
Arguments:
- queries: bfloat16 [2048, 4096], P('dp', 'grp'), may hold values from -6 to 6
- passages: bfloat16 [16, 128, 4096], P(None, 'dp', 'grp'), may hold values from -6 to 6
- block_lists: int32 [16, 3], P('dp'), may hold values from 0 to 15
- list_lengths: int32 [16], P('dp'), may hold values from 1 to 3, as said below
- positive: int32 [2048], P('dp'), may hold values from 0 to 2047, as said below
- loss_grad: float32 [2048], P('dp'), may hold values from -16 to 16
Outputs:
- losses: float32 [2048], P('dp')
- grad_queries: bfloat16 [2048, 4096], P('dp', 'grp')
- grad_passages: bfloat16 [16, 128, 4096], P(None, 'dp', 'grp')
The draws below stay inside these ranges and needn't reach their ends.
Inputs may be any that keep to these rules, and one draw needn't show every extreme that they name: `block_lists`: entries of a list past its length are ignored. `list_lengths`: the 2 query blocks of one dp index list 4 blocks or fewer together; in every draw some dp index lists exactly 4, with one of its blocks listing 3. positive[q] = n * 128 + r with r // 16 == q // 256.
All inputs are finite; a program needn't handle non-finite values.
Results may differ from the reference program's by a relative error of at most 0.0052.
Values may be sent and summed in bfloat16 or wider, within the bound.
No kernel may reach another device: no remote copies, remote signals or barrier semaphores. Data moves between devices by JAX's collectives and lax.ppermute only.
A program may use at most 64 MiB of HBM per device.

```python
import math
import jax
import jax.numpy as jnp
from jax import lax

D = 4096
BLOCK = 128
LIST_MAX = 3
QB_DEV = 2
NQB = 16
NQ = 2048
NPB = 16
LIVE_MAX = 4
N_DP = 8


def draw_queries(key, part):
    noise = jax.random.normal(jax.random.fold_in(key, 1), (NQ, D), jnp.float32)
    values = noise
    return jnp.clip(values, -6.0, 6.0).astype(jnp.bfloat16)


def draw_passages(key, part):
    noise = jax.random.normal(jax.random.fold_in(key, 5), (NPB, BLOCK, D), jnp.float32)
    values = noise
    return jnp.clip(values, -6.0, 6.0).astype(jnp.bfloat16)


def draw_list_lengths(key, part):
    owners = NQB // QB_DEV
    budget = LIVE_MAX - QB_DEV
    extra_raw = jax.random.randint(jax.random.fold_in(key, 1), (owners, QB_DEV), 0, LIST_MAX)
    running = jnp.cumsum(extra_raw, axis=1) - extra_raw
    room = jnp.maximum(budget - running, 0)
    extras = jnp.minimum(extra_raw, room)
    heavy = jax.random.randint(jax.random.fold_in(key, 2), (), 0, owners)
    ranking = jax.random.permutation(jax.random.fold_in(key, 3), QB_DEV).astype(jnp.int32)
    heavy_extras = jnp.clip(budget - (LIST_MAX - 1) * ranking, 0, LIST_MAX - 1)
    owner_index = jnp.arange(owners, dtype=jnp.int32)[:, None]
    extras = jnp.where(owner_index == heavy, heavy_extras[None, :], extras)
    return (1 + extras).reshape(NQB).astype(jnp.int32)


def draw_positive(key, part):
    owners = NQB // QB_DEV
    shard_rows = BLOCK // owners
    query_owner = jnp.arange(NQ, dtype=jnp.int32) // (QB_DEV * BLOCK)
    block_pick = jax.random.randint(jax.random.fold_in(key, 1), (NQ,), 0, NPB)
    row_pick = jax.random.randint(jax.random.fold_in(key, 2), (NQ,), 0, shard_rows)
    return (block_pick * BLOCK + query_owner * shard_rows + row_pick).astype(jnp.int32)


def plant(array, own_key, smallest, high):
    longest = array.shape.index(max(array.shape))
    spots = []
    for shift in (0, 1):
        where = [jax.random.randint(jax.random.fold_in(own_key, axis), (), 0, length) for axis, length in enumerate(array.shape)]
        where[longest] = (where[longest] + shift) % array.shape[longest]
        spots.append(tuple(where))
    return array.at[spots[0]].set(smallest).at[spots[1]].set(high)


def steps_of(rng, extent, pieces, smallest, largest):
    def one(dim, blocks):
        heights = jax.random.uniform(jax.random.fold_in(jax.random.fold_in(rng, 6), dim), (blocks,), jnp.float32, smallest / len(pieces), largest / len(pieces))
        return jnp.repeat(jnp.exp(heights), extent[dim] // blocks).reshape((-1,) + (1,) * (len(extent) - dim - 1))

    loudness = one(*pieces[0])
    for cut in pieces[1:]:
        loudness = loudness * one(*cut)
    return loudness


def scatter_about(stream_key, shape, scale, reach, cuts=(), held_as=jnp.bfloat16):
    level = steps_of(stream_key, shape, cuts, -0.22, 0.18) if cuts else 1.0
    result = jax.random.normal(stream_key, shape, jnp.float32) * scale * level
    return jnp.minimum(jnp.maximum(result, -reach), reach).astype(held_as)


def setup_inputs(seed: int = 0) -> dict:
    key_list = jax.random.split(jax.random.key(seed), 7)
    return {
        "queries": draw_queries(jax.random.fold_in(key_list[6], 71), 0),
        "passages": draw_passages(jax.random.fold_in(key_list[6], 71), 0),
        "block_lists": plant(jax.random.randint(key_list[2], (NQB, LIST_MAX), 0, NPB), jax.random.fold_in(key_list[2], 1), 0, NPB - 1).astype(jnp.int32),
        "list_lengths": draw_list_lengths(jax.random.fold_in(key_list[6], 71), 0),
        "positive": draw_positive(jax.random.fold_in(key_list[6], 71), 0),
        "loss_grad": scatter_about(key_list[5], (NQ,), 4.0, 16.0, ((0, 8),), jnp.float32),
    }


def reference(queries, passages, block_lists, list_lengths, positive, loss_grad):
    score_scale = 3.0 / math.sqrt(D)
    shard_rows = BLOCK // N_DP
    query_rows = QB_DEV * BLOCK
    block_total = passages.shape[0]
    entry_index = jnp.arange(LIST_MAX, dtype=jnp.int32)
    column_index = jnp.arange(block_total * shard_rows, dtype=jnp.int32)

    def owner_step(carry, dp_owner):
        first = dp_owner * query_rows
        own_queries = lax.dynamic_slice_in_dim(queries, first, query_rows, 0)
        own_positive = lax.dynamic_slice_in_dim(positive, first, query_rows, 0)
        own_grad = lax.dynamic_slice_in_dim(loss_grad, first, query_rows, 0)
        own_lists = lax.dynamic_slice_in_dim(block_lists, dp_owner * QB_DEV, QB_DEV, 0)
        own_lengths = lax.dynamic_slice_in_dim(list_lengths, dp_owner * QB_DEV, QB_DEV, 0)
        row_start = dp_owner * shard_rows
        in_batch = lax.dynamic_slice_in_dim(passages, row_start, shard_rows, 1)
        in_flat = in_batch.reshape(block_total * shard_rows, D)
        scores_in = score_scale * jnp.dot(own_queries, in_flat.T, preferred_element_type=jnp.float32)
        listed = passages[own_lists.reshape(-1)].reshape(QB_DEV, LIST_MAX, BLOCK, D).astype(jnp.float32)
        query_blocks = own_queries.reshape(QB_DEV, BLOCK, D).astype(jnp.float32)
        scores_list = score_scale * jnp.einsum('bqf,blpf->bqlp', query_blocks, listed)
        slot_live = (entry_index[None, :] < own_lengths[:, None])[:, None, :, None]
        list_peak = lax.optimization_barrier(jnp.max(jnp.where(slot_live, scores_list, -jnp.inf), axis=(2, 3))).reshape(query_rows)
        row_peak = jnp.maximum(lax.optimization_barrier(jnp.max(scores_in, axis=1)), list_peak)
        peak_blocks = row_peak.reshape(QB_DEV, BLOCK, 1, 1)
        list_total = lax.optimization_barrier(jnp.sum(jnp.where(slot_live, jnp.exp(scores_list - peak_blocks), 0.0), axis=(2, 3))).reshape(query_rows)
        row_total = lax.optimization_barrier(jnp.sum(jnp.exp(scores_in - row_peak[:, None]), axis=1)) + list_total
        log_total = row_peak + jnp.log(row_total)
        pos_column = own_positive // BLOCK * shard_rows + own_positive % BLOCK - row_start
        is_positive = column_index[None, :] == pos_column[:, None]
        positive_score = lax.optimization_barrier(jnp.sum(jnp.where(is_positive, scores_in, 0.0), axis=1))
        losses = log_total - positive_score
        weights_in = (own_grad[:, None] * (jnp.exp(scores_in - log_total[:, None]) - is_positive.astype(jnp.float32))).astype(jnp.bfloat16)
        log_blocks = log_total.reshape(QB_DEV, BLOCK, 1, 1)
        grad_blocks = own_grad.reshape(QB_DEV, BLOCK, 1, 1)
        weights_list = jnp.where(slot_live, grad_blocks * jnp.exp(scores_list - log_blocks), 0.0).astype(jnp.bfloat16)
        near_terms = jnp.dot(weights_in, in_flat, preferred_element_type=jnp.float32)
        far_terms = jnp.einsum('bqlp,blpf->bqf', weights_list.astype(jnp.float32), listed).reshape(query_rows, D)
        grad_queries = (score_scale * (near_terms + far_terms)).astype(jnp.bfloat16)
        own_part = score_scale * jnp.dot(weights_in.T, own_queries, preferred_element_type=jnp.float32)
        shares = (score_scale * jnp.einsum('bqlp,bqf->blpf', weights_list.astype(jnp.float32), query_blocks)).astype(jnp.bfloat16)
        current = lax.dynamic_slice_in_dim(carry, row_start, shard_rows, 1)
        carry = lax.dynamic_update_slice_in_dim(carry, current + own_part.reshape(block_total, shard_rows, D), row_start, 1)
        carry = carry.at[own_lists.reshape(-1)].add(shares.reshape(QB_DEV * LIST_MAX, BLOCK, D).astype(jnp.float32))
        return (carry, (losses, grad_queries))
    start = jnp.zeros((block_total, BLOCK, D), jnp.float32)
    summed, outputs = lax.scan(owner_step, start, jnp.arange(N_DP, dtype=jnp.int32))
    losses, grad_queries = outputs
    return (losses.reshape(-1), grad_queries.reshape(-1, D), summed.astype(jnp.bfloat16))
```

```python
import functools
import math

import jax
import jax.numpy as jnp
from jax import lax
from jax.experimental import pallas as pl
from jax.experimental.pallas import tpu as pltpu
from jax.sharding import PartitionSpec as P

D = 4096
LIVE_MAX = 4


def pick_rows(selector, table):
    return jnp.sum(jnp.where(selector[:, :, None], table[None], 0.0), axis=1)


def exchange_plan(queries, passages, block_lists, list_lengths, positive, loss_grad):
    score_scale = 3.0 / math.sqrt(D)
    dp_count = lax.axis_size("dp")
    dp_owner = lax.axis_index("dp")
    block_count, list_cap = block_lists.shape
    block_total, shard_rows, feature_width = passages.shape
    block_size = shard_rows * dp_count
    query_rows = queries.shape[0]
    query_blocks = queries.reshape(block_count, block_size, feature_width)
    entry_index = jnp.arange(list_cap, dtype=jnp.int32)
    block_index = jnp.arange(block_count, dtype=jnp.int32)
    slot_count = LIVE_MAX
    slot_index = jnp.arange(slot_count, dtype=jnp.int32)
    list_ends = jnp.cumsum(list_lengths)
    list_starts = list_ends - list_lengths
    slot_block = jnp.minimum(
        jnp.sum((list_ends[None, :] <= slot_index[:, None]).astype(jnp.int32), axis=1),
        block_count - 1,
    )
    owner_match = slot_block[:, None] == block_index[None, :]
    offset = slot_index - jnp.sum(jnp.where(owner_match, list_starts[None, :], 0), axis=1)
    slot_live = slot_index < list_ends[block_count - 1]
    entry_match = owner_match[:, :, None] & (offset[:, None, None] == entry_index[None, None, :])
    slot_ids = jnp.sum(jnp.where(entry_match, block_lists[None], 0), axis=(1, 2))
    all_ids = lax.all_gather(slot_ids, "dp", axis=0, tiled=True)
    outgoing = passages[all_ids].reshape(dp_count, slot_count, shard_rows, feature_width)
    fetched = lax.all_to_all(outgoing, "dp", split_axis=0, concat_axis=2, tiled=True).reshape(
        slot_count, block_size, feature_width
    )
    local_rows = passages.reshape(block_total * shard_rows, feature_width)
    block_match = slot_block[:, None] == block_index[None, :]
    chosen = jnp.einsum(
        "sb,bqf->sqf",
        block_match.astype(jnp.bfloat16),
        query_blocks,
        preferred_element_type=jnp.float32,
    ).astype(jnp.bfloat16)
    part_in = lax.dot_general(
        queries, local_rows, (((1,), (1,)), ((), ())), preferred_element_type=jnp.float32
    )
    part_list = jnp.einsum("sqf,spf->sqp", chosen, fetched, preferred_element_type=jnp.float32)
    full_in, full_list = lax.psum((part_in, part_list), "grp")
    scores_in = score_scale * full_in
    scores_list = score_scale * full_list
    slot_open = block_match & slot_live[:, None]
    slot_peak = jnp.max(scores_list, axis=2)
    list_peak = jnp.max(
        jnp.where(slot_open[:, :, None], slot_peak[:, None, :], -jnp.inf), axis=0
    ).reshape(query_rows)
    row_peak = jnp.maximum(jnp.max(scores_in, axis=1), list_peak)
    slot_shift = pick_rows(block_match, row_peak.reshape(block_count, block_size))
    slot_sums = jnp.sum(jnp.exp(scores_list - slot_shift[:, :, None]), axis=2)
    list_total = jnp.sum(
        jnp.where(slot_open[:, :, None], slot_sums[:, None, :], 0.0), axis=0
    ).reshape(query_rows)
    row_total = jnp.sum(jnp.exp(scores_in - row_peak[:, None]), axis=1) + list_total
    log_total = row_peak + jnp.log(row_total)
    pos_column = positive // block_size * shard_rows + positive % block_size - dp_owner * shard_rows
    column_index = jnp.arange(block_total * shard_rows, dtype=jnp.int32)
    is_positive = column_index[None, :] == pos_column[:, None]
    positive_score = jnp.sum(jnp.where(is_positive, scores_in, 0.0), axis=1)
    losses = log_total - positive_score
    weights_in = (
        loss_grad[:, None]
        * (jnp.exp(scores_in - log_total[:, None]) - is_positive.astype(jnp.float32))
    ).astype(jnp.bfloat16)
    slot_log = pick_rows(block_match, log_total.reshape(block_count, block_size))
    slot_grad = pick_rows(block_match, loss_grad.reshape(block_count, block_size))
    weights_list = jnp.where(
        slot_live[:, None, None],
        slot_grad[:, :, None] * jnp.exp(scores_list - slot_log[:, :, None]),
        0.0,
    ).astype(jnp.bfloat16)
    near_terms = jnp.dot(weights_in, local_rows, preferred_element_type=jnp.float32)
    per_slot = jnp.einsum("sqp,spf->sqf", weights_list, fetched, preferred_element_type=jnp.float32)
    far_terms = jnp.einsum(
        "sb,sqf->bqf", block_match.astype(jnp.float32), per_slot, precision=lax.Precision.HIGHEST
    ).reshape(query_rows, feature_width)
    grad_queries = (score_scale * (near_terms + far_terms)).astype(jnp.bfloat16)
    shares = (
        score_scale
        * jnp.einsum("sqp,sqf->spf", weights_list, chosen, preferred_element_type=jnp.float32)
    ).astype(jnp.bfloat16)
    returned = lax.all_to_all(
        shares.reshape(1, slot_count, block_size, feature_width),
        "dp",
        split_axis=2,
        concat_axis=0,
        tiled=True,
    )
    own_part = score_scale * lax.dot_general(
        weights_in, queries, (((0,), (0,)), ((), ())), preferred_element_type=jnp.float32
    )
    summed = (
        own_part.reshape(block_total, shard_rows, feature_width)
        .at[all_ids]
        .add(returned.reshape(dp_count * slot_count, shard_rows, feature_width).astype(jnp.float32))
    )
    return (losses, grad_queries, summed.astype(jnp.bfloat16))


def power_of_two(count):
    return count > 0 and count & (count - 1) == 0


def pairwise_fits(passage_shape, list_shape):
    dp_count, grp_count = lax.axis_size("dp"), lax.axis_size("grp")
    block_total, shard_rows, feature_width = passage_shape
    block_size = shard_rows * dp_count
    return (
        power_of_two(dp_count)
        and power_of_two(grp_count)
        and grp_count > 1
        and shard_rows % 16 == 0
        and block_size % 128 == 0
        and feature_width % 128 == 0
        and (block_total * shard_rows) % 256 == 0
        and LIVE_MAX % 2 == 0
    )


def swap(value, axis, bit):
    return lax.ppermute(value, axis, [(i, i ^ bit) for i in range(lax.axis_size(axis))])


def sum_over_grp(keep, send):
    half = keep + swap(send, "grp", 1)
    bit = 2
    while bit < lax.axis_size("grp"):
        half = half + swap(half, "grp", bit)
        bit *= 2
    return half, swap(half, "grp", 1)


class Lists:
    def __init__(self, table, block_count, list_cap):
        self.table, self.block_count, self.list_cap = table, block_count, list_cap
        self.width = block_count * (1 + list_cap)

    def slot(self, owner, s):
        base = owner * self.width
        end, start, block, live = 0, 0, 0, False
        for b in range(self.block_count):
            begin = end
            end = end + self.table[base + b]
            inside = s >= begin
            block = jnp.where(inside, b, block)
            start = jnp.where(inside, begin, start)
            live = s < end
        entry = jnp.minimum(s - start, self.list_cap - 1)
        listed = self.table[base + self.block_count + block * self.list_cap + entry]
        return block, jnp.where(live, listed, 0), live


def gather_kernel(lists_of, slots, table, passages, *pieces):
    lists = lists_of(table)
    me = lax.axis_index("dp")
    for k, piece in enumerate(pieces):
        for s in range(slots):
            _, listed, _ = lists.slot(me ^ k, s)
            piece[s] = passages[listed]


NT = (((1,), (1,)), ((), ()))
TN = (((0,), (0,)), ((), ()))


def dot(a, b, dims=(((1,), (0,)), ((), ()))):
    return lax.dot_general(a, b, dims, preferred_element_type=jnp.float32)


def own_scores_kernel(local, queries, keep, send):
    rows = keep.shape[0]
    core = lax.axis_index("grp") & 1
    q = queries[...]
    keep[...] = dot(local[pl.ds(core * rows, rows), :], q, NT)
    send[...] = dot(local[pl.ds((1 - core) * rows, rows), :], q, NT)


def listed_scores_kernel(lists_of, table, queries, *refs):
    pieces, (keep, send) = refs[:-2], refs[-2:]
    lists = lists_of(table)
    me = lax.axis_index("dp")
    core = lax.axis_index("grp") & 1
    count, block_size = keep.shape[0], keep.shape[1]
    for out, first in ((keep, core * count), (send, (1 - core) * count)):
        for i in range(count):
            block, _, _ = lists.slot(me, first + i)
            rows = jnp.concatenate([piece[first + i] for piece in pieces], axis=0)
            out[i] = dot(rows, queries[pl.ds(block * block_size, block_size), :], NT)


def weights_kernel(
    lists_of, scale, table, in_half, in_other, list_half, list_other, queries, pos_column,
    loss_grad, losses, weights_in, weights_list, *refs
):
    shares, (scores_in, scores_list) = refs[:-2], refs[-2:]
    lists = lists_of(table)
    me = lax.axis_index("dp")
    core = lax.axis_index("grp") & 1
    rows, count = in_half.shape[0], list_half.shape[0]
    slots, block_size = scores_list.shape[0], scores_list.shape[1]
    shard_rows = shares[0].shape[1]
    blocks = lists.block_count
    scores_in[pl.ds(core * rows, rows), :] = scale * in_half[...]
    scores_in[pl.ds((1 - core) * rows, rows), :] = scale * in_other[...]
    scores_list[pl.ds(core * count, count)] = scale * list_half[...]
    scores_list[pl.ds((1 - core) * count, count)] = scale * list_other[...]
    info = [lists.slot(me, s) for s in range(slots)]
    near = scores_in[...]
    listed = [scores_list[s] for s in range(slots)]

    def of_slot(values, s):
        picked = values[0]
        for b in range(1, blocks):
            picked = jnp.where(info[s][0] == b, values[b], picked)
        return picked

    def by_block(row):
        return [row[:, b * block_size : (b + 1) * block_size] for b in range(blocks)]

    in_block = [[(info[s][0] == b) & info[s][2] for s in range(slots)] for b in range(blocks)]
    peaks = by_block(jnp.max(near, axis=0, keepdims=True))
    slot_peaks = [jnp.max(x, axis=0, keepdims=True) for x in listed]
    for b in range(blocks):
        for s in range(slots):
            peaks[b] = jnp.maximum(peaks[b], jnp.where(in_block[b][s], slot_peaks[s], -jnp.inf))
    row_peak = jnp.concatenate(peaks, axis=1)
    totals = by_block(jnp.sum(jnp.exp(near - row_peak), axis=0, keepdims=True))
    slot_sums = [
        jnp.sum(jnp.exp(listed[s] - of_slot(peaks, s)), axis=0, keepdims=True) for s in range(slots)
    ]
    for b in range(blocks):
        for s in range(slots):
            totals[b] = totals[b] + jnp.where(in_block[b][s], slot_sums[s], 0.0)
    log_total = row_peak + jnp.log(jnp.concatenate(totals, axis=1))
    is_positive = lax.broadcasted_iota(jnp.int32, near.shape, 0) == pos_column[...]
    positive_score = jnp.sum(jnp.where(is_positive, near, 0.0), axis=0, keepdims=True)
    losses[...] = log_total - positive_score
    grad = loss_grad[...]
    weights_in[...] = (
        grad * (jnp.exp(near - log_total) - is_positive.astype(jnp.float32))
    ).astype(jnp.bfloat16)
    logs, grads = by_block(log_total), by_block(grad)
    for s in range(slots):
        weight = jnp.where(
            info[s][2], of_slot(grads, s) * jnp.exp(listed[s] - of_slot(logs, s)), 0.0
        ).astype(jnp.bfloat16)
        weights_list[s] = weight
        q = queries[pl.ds(info[s][0] * block_size, block_size), :]
        share = (scale * dot(weight, q)).astype(jnp.bfloat16)
        for k, out in enumerate(shares):
            out[s] = share[k * shard_rows : (k + 1) * shard_rows]


def own_grads_kernel(
    lists_of, scale, table, weights_in, weights_list, queries, local, own_share, *refs
):
    pieces, (grad_queries, own_part, total) = refs[:-3], refs[-3:]
    lists = lists_of(table)
    me = lax.axis_index("dp")
    slots, block_size = weights_list.shape[0], weights_list.shape[1]
    shard_rows = own_share.shape[1]
    near = weights_in[...]
    total[...] = dot(near, local[...], TN)
    own_part[...] = scale * dot(near, queries[...])
    for s in range(slots):
        block, listed, _ = lists.slot(me, s)
        rows = jnp.concatenate([piece[s] for piece in pieces], axis=0)
        at = pl.ds(block * block_size, block_size)
        total[at, :] = total[at, :] + dot(weights_list[s], rows, TN)
        at = pl.ds(listed * shard_rows, shard_rows)
        own_part[at, :] = own_part[at, :] + own_share[s].astype(jnp.float32)
    grad_queries[...] = (scale * total[...]).astype(jnp.bfloat16)


def collect_kernel(lists_of, table, own_part, *refs):
    returned, (grad_passages, total) = refs[:-2], refs[-2:]
    lists = lists_of(table)
    me = lax.axis_index("dp")
    slots, shard_rows = returned[0].shape[0], returned[0].shape[1]
    total[...] = own_part[...]
    for k, piece in enumerate(returned):
        for s in range(slots):
            _, listed, _ = lists.slot(me ^ (k + 1), s)
            at = pl.ds(listed * shard_rows, shard_rows)
            total[at, :] = total[at, :] + piece[s].astype(jnp.float32)
    grad_passages[...] = total[...].astype(jnp.bfloat16)


def local_call(kernel, outs, scratch=(), table=True, name=None):
    shapes = [jax.ShapeDtypeStruct(shape, dtype) for shape, dtype in outs]

    def call(*args):
        smem = [pl.BlockSpec(memory_space=pltpu.SMEM)] if table else []
        vmem = pl.BlockSpec(memory_space=pltpu.VMEM)
        return pl.pallas_call(
            kernel,
            out_shape=shapes,
            in_specs=smem + [vmem] * (len(args) - len(smem)),
            out_specs=[vmem] * len(shapes),
            scratch_shapes=[pltpu.VMEM(shape, dtype) for shape, dtype in scratch],
            name=name,
        )(*args)

    return call


def pairwise_plan(queries, passages, block_lists, list_lengths, positive, loss_grad):
    bf16, f32 = jnp.bfloat16, jnp.float32
    scale = 3.0 / math.sqrt(D)
    dp_count, me = lax.axis_size("dp"), lax.axis_index("dp")
    block_count, list_cap = block_lists.shape
    block_total, shard_rows, width = passages.shape
    block_size = shard_rows * dp_count
    query_rows = queries.shape[0]
    own_rows = block_total * shard_rows
    slots = LIVE_MAX
    peers = range(1, dp_count)
    lists_of = functools.partial(Lists, block_count=block_count, list_cap=list_cap)

    mine = jnp.concatenate([list_lengths, block_lists.reshape(-1)])
    placed = jnp.where(jnp.arange(dp_count)[:, None] == me, mine[None], 0)
    table = lax.psum(placed.reshape(-1), "dp")

    local = passages.reshape(own_rows, width)
    in_half = ((own_rows // 2, query_rows), f32)
    keep_in, send_in = local_call(
        own_scores_kernel, [in_half, in_half], table=False, name="own_scores"
    )(local, queries)

    piece = ((slots, shard_rows, width), bf16)
    outgoing = local_call(
        functools.partial(gather_kernel, lists_of, slots), [piece] * dp_count, name="gather"
    )(table, passages)
    fetched = [outgoing[0]] + [None] * (dp_count - 1)
    for k in reversed(peers):
        fetched[k] = swap(outgoing[k], "dp", k)
    in_sums = sum_over_grp(keep_in, send_in)

    list_half = ((slots // 2, block_size, block_size), f32)
    keep_list, send_list = local_call(
        functools.partial(listed_scores_kernel, lists_of), [list_half, list_half], name="listed_scores"
    )(table, queries, *fetched)
    list_sums = sum_over_grp(keep_list, send_list)

    pos_column = positive // block_size * shard_rows + positive % block_size - me * shard_rows
    losses, weights_in, weights_list, *shares = local_call(
        functools.partial(weights_kernel, lists_of, scale),
        [
            ((1, query_rows), f32),
            ((own_rows, query_rows), bf16),
            ((slots, block_size, block_size), bf16),
        ]
        + [piece] * dp_count,
        scratch=[((own_rows, query_rows), f32), ((slots, block_size, block_size), f32)],
        name="weights",
    )(
        table, *in_sums, *list_sums, queries,
        pos_column.reshape(1, query_rows), loss_grad.reshape(1, query_rows),
    )
    returned = [None] * dp_count
    for k in reversed(peers):
        returned[k] = swap(shares[k], "dp", k)

    grad_queries, own_part = local_call(
        functools.partial(own_grads_kernel, lists_of, scale),
        [((query_rows, width), bf16), ((own_rows, width), f32)],
        scratch=[((query_rows, width), f32)],
        name="own_grads",
    )(table, weights_in, weights_list, queries, local, shares[0], *fetched)
    (grad_passages,) = local_call(
        functools.partial(collect_kernel, lists_of),
        [((own_rows, width), bf16)],
        scratch=[((own_rows, width), f32)],
        name="collect",
    )(table, own_part, *returned[1:])
    return (
        losses.reshape(query_rows),
        grad_queries,
        grad_passages.reshape(block_total, shard_rows, width),
    )


def per_device(queries, passages, block_lists, list_lengths, positive, loss_grad):
    plan = pairwise_plan if pairwise_fits(passages.shape, block_lists.shape) else exchange_plan
    return plan(queries, passages, block_lists, list_lengths, positive, loss_grad)


def solution(mesh):
    in_specs = (P("dp", "grp"), P(None, "dp", "grp"), P("dp", None), P("dp"), P("dp"), P("dp"))
    out_specs = (P("dp"), P("dp", "grp"), P(None, "dp", "grp"))
    return jax.shard_map(
        per_device, mesh=mesh, in_specs=in_specs, out_specs=out_specs, check_vma=False
    )
```

```python
import functools
import math

import jax
import jax.numpy as jnp
from jax import lax
from jax.experimental import pallas as pl
from jax.experimental.pallas import tpu as pltpu
from jax.sharding import PartitionSpec as P

D = 4096
LIVE_MAX = 4


def pick_rows(selector, table):
    return jnp.sum(jnp.where(selector[:, :, None], table[None], 0.0), axis=1)


def exchange_plan(queries, passages, block_lists, list_lengths, positive, loss_grad):
    score_scale = 3.0 / math.sqrt(D)
    dp_count = lax.axis_size("dp")
    dp_owner = lax.axis_index("dp")
    block_count, list_cap = block_lists.shape
    block_total, shard_rows, feature_width = passages.shape
    block_size = shard_rows * dp_count
    query_rows = queries.shape[0]
    query_blocks = queries.reshape(block_count, block_size, feature_width)
    entry_index = jnp.arange(list_cap, dtype=jnp.int32)
    block_index = jnp.arange(block_count, dtype=jnp.int32)
    slot_count = LIVE_MAX
    slot_index = jnp.arange(slot_count, dtype=jnp.int32)
    list_ends = jnp.cumsum(list_lengths)
    list_starts = list_ends - list_lengths
    slot_block = jnp.minimum(
        jnp.sum((list_ends[None, :] <= slot_index[:, None]).astype(jnp.int32), axis=1),
        block_count - 1,
    )
    owner_match = slot_block[:, None] == block_index[None, :]
    offset = slot_index - jnp.sum(jnp.where(owner_match, list_starts[None, :], 0), axis=1)
    slot_live = slot_index < list_ends[block_count - 1]
    entry_match = owner_match[:, :, None] & (offset[:, None, None] == entry_index[None, None, :])
    slot_ids = jnp.sum(jnp.where(entry_match, block_lists[None], 0), axis=(1, 2))
    all_ids = lax.all_gather(slot_ids, "dp", axis=0, tiled=True)
    outgoing = passages[all_ids].reshape(dp_count, slot_count, shard_rows, feature_width)
    fetched = lax.all_to_all(outgoing, "dp", split_axis=0, concat_axis=2, tiled=True).reshape(
        slot_count, block_size, feature_width
    )
    local_rows = passages.reshape(block_total * shard_rows, feature_width)
    block_match = slot_block[:, None] == block_index[None, :]
    chosen = jnp.einsum(
        "sb,bqf->sqf",
        block_match.astype(jnp.bfloat16),
        query_blocks,
        preferred_element_type=jnp.float32,
    ).astype(jnp.bfloat16)
    part_in = lax.dot_general(
        queries, local_rows, (((1,), (1,)), ((), ())), preferred_element_type=jnp.float32
    )
    part_list = jnp.einsum("sqf,spf->sqp", chosen, fetched, preferred_element_type=jnp.float32)
    full_in, full_list = lax.psum((part_in, part_list), "grp")
    scores_in = score_scale * full_in
    scores_list = score_scale * full_list
    slot_open = block_match & slot_live[:, None]
    slot_peak = jnp.max(scores_list, axis=2)
    list_peak = jnp.max(
        jnp.where(slot_open[:, :, None], slot_peak[:, None, :], -jnp.inf), axis=0
    ).reshape(query_rows)
    row_peak = jnp.maximum(jnp.max(scores_in, axis=1), list_peak)
    slot_shift = pick_rows(block_match, row_peak.reshape(block_count, block_size))
    slot_sums = jnp.sum(jnp.exp(scores_list - slot_shift[:, :, None]), axis=2)
    list_total = jnp.sum(
        jnp.where(slot_open[:, :, None], slot_sums[:, None, :], 0.0), axis=0
    ).reshape(query_rows)
    row_total = jnp.sum(jnp.exp(scores_in - row_peak[:, None]), axis=1) + list_total
    log_total = row_peak + jnp.log(row_total)
    pos_column = positive // block_size * shard_rows + positive % block_size - dp_owner * shard_rows
    column_index = jnp.arange(block_total * shard_rows, dtype=jnp.int32)
    is_positive = column_index[None, :] == pos_column[:, None]
    positive_score = jnp.sum(jnp.where(is_positive, scores_in, 0.0), axis=1)
    losses = log_total - positive_score
    weights_in = (
        loss_grad[:, None]
        * (jnp.exp(scores_in - log_total[:, None]) - is_positive.astype(jnp.float32))
    ).astype(jnp.bfloat16)
    slot_log = pick_rows(block_match, log_total.reshape(block_count, block_size))
    slot_grad = pick_rows(block_match, loss_grad.reshape(block_count, block_size))
    weights_list = jnp.where(
        slot_live[:, None, None],
        slot_grad[:, :, None] * jnp.exp(scores_list - slot_log[:, :, None]),
        0.0,
    ).astype(jnp.bfloat16)
    near_terms = jnp.dot(weights_in, local_rows, preferred_element_type=jnp.float32)
    per_slot = jnp.einsum("sqp,spf->sqf", weights_list, fetched, preferred_element_type=jnp.float32)
    far_terms = jnp.einsum(
        "sb,sqf->bqf", block_match.astype(jnp.float32), per_slot, precision=lax.Precision.HIGHEST
    ).reshape(query_rows, feature_width)
    grad_queries = (score_scale * (near_terms + far_terms)).astype(jnp.bfloat16)
    shares = (
        score_scale
        * jnp.einsum("sqp,sqf->spf", weights_list, chosen, preferred_element_type=jnp.float32)
    ).astype(jnp.bfloat16)
    returned = lax.all_to_all(
        shares.reshape(1, slot_count, block_size, feature_width),
        "dp",
        split_axis=2,
        concat_axis=0,
        tiled=True,
    )
    own_part = score_scale * lax.dot_general(
        weights_in, queries, (((0,), (0,)), ((), ())), preferred_element_type=jnp.float32
    )
    summed = (
        own_part.reshape(block_total, shard_rows, feature_width)
        .at[all_ids]
        .add(returned.reshape(dp_count * slot_count, shard_rows, feature_width).astype(jnp.float32))
    )
    return (losses, grad_queries, summed.astype(jnp.bfloat16))


KERNEL_VMEM = 8 * 1024 * 1024


def power_of_two(count):
    return count > 0 and count & (count - 1) == 0


def pairwise_fits(passage_shape, list_shape):
    dp_count, grp_count = lax.axis_size("dp"), lax.axis_size("grp")
    block_total, shard_rows, feature_width = passage_shape
    block_size = shard_rows * dp_count
    return (
        power_of_two(dp_count)
        and power_of_two(grp_count)
        and grp_count > 1
        and shard_rows % 16 == 0
        and block_size % 128 == 0
        and feature_width % 128 == 0
        and (block_total * shard_rows) % 256 == 0
        and LIVE_MAX % 2 == 0
    )


def swap(value, axis, bit):
    return lax.ppermute(value, axis, [(i, i ^ bit) for i in range(lax.axis_size(axis))])


def sum_over_grp(keep, send):
    half = keep + swap(send, "grp", 1)
    bit = 2
    while bit < lax.axis_size("grp"):
        half = half + swap(half, "grp", bit)
        bit *= 2
    return half, swap(half, "grp", 1)


class Lists:
    def __init__(self, table, block_count, list_cap):
        self.table, self.block_count, self.list_cap = table, block_count, list_cap
        self.width = block_count * (1 + list_cap)

    def slot(self, owner, s):
        base = owner * self.width
        end, start, block, live = 0, 0, 0, False
        for b in range(self.block_count):
            begin = end
            end = end + self.table[base + b]
            inside = s >= begin
            block = jnp.where(inside, b, block)
            start = jnp.where(inside, begin, start)
            live = s < end
        entry = jnp.minimum(s - start, self.list_cap - 1)
        listed = self.table[base + self.block_count + block * self.list_cap + entry]
        return block, jnp.where(live, listed, 0), live


def gather_kernel(lists_of, slots, table, passages, *pieces):
    lists = lists_of(table)
    me = lax.axis_index("dp")
    for k, piece in enumerate(pieces):
        for s in range(slots):
            _, listed, _ = lists.slot(me ^ k, s)
            piece[s] = passages[listed]


NT = (((1,), (1,)), ((), ()))
TN = (((0,), (0,)), ((), ()))


def dot(a, b, dims=(((1,), (0,)), ((), ()))):
    return lax.dot_general(a, b, dims, preferred_element_type=jnp.float32)


def own_scores_kernel(local, queries, keep, send):
    rows = keep.shape[0]
    core = lax.axis_index("grp") & 1
    q = queries[...]
    keep[...] = dot(local[pl.ds(core * rows, rows), :], q, NT)
    send[...] = dot(local[pl.ds((1 - core) * rows, rows), :], q, NT)


def listed_scores_kernel(lists_of, table, queries, *refs):
    pieces, (keep, send) = refs[:-2], refs[-2:]
    lists = lists_of(table)
    me = lax.axis_index("dp")
    core = lax.axis_index("grp") & 1
    count, block_size = keep.shape[0], keep.shape[1]
    for out, first in ((keep, core * count), (send, (1 - core) * count)):
        for i in range(count):
            block, _, _ = lists.slot(me, first + i)
            rows = jnp.concatenate([piece[first + i] for piece in pieces], axis=0)
            out[i] = dot(rows, queries[pl.ds(block * block_size, block_size), :], NT)


def weights_kernel(
    lists_of, scale, table, in_half, in_other, list_half, list_other, queries, pos_column,
    loss_grad, losses, weights_in, weights_list, *refs
):
    shares, (scores_in, scores_list) = refs[:-2], refs[-2:]
    lists = lists_of(table)
    me = lax.axis_index("dp")
    core = lax.axis_index("grp") & 1
    rows, count = in_half.shape[0], list_half.shape[0]
    slots, block_size = scores_list.shape[0], scores_list.shape[1]
    shard_rows = shares[0].shape[1]
    blocks = lists.block_count
    scores_in[pl.ds(core * rows, rows), :] = scale * in_half[...]
    scores_in[pl.ds((1 - core) * rows, rows), :] = scale * in_other[...]
    scores_list[pl.ds(core * count, count)] = scale * list_half[...]
    scores_list[pl.ds((1 - core) * count, count)] = scale * list_other[...]
    info = [lists.slot(me, s) for s in range(slots)]
    near = scores_in[...]
    listed = [scores_list[s] for s in range(slots)]

    def of_slot(values, s):
        picked = values[0]
        for b in range(1, blocks):
            picked = jnp.where(info[s][0] == b, values[b], picked)
        return picked

    def by_block(row):
        return [row[:, b * block_size : (b + 1) * block_size] for b in range(blocks)]

    in_block = [[(info[s][0] == b) & info[s][2] for s in range(slots)] for b in range(blocks)]
    peaks = by_block(jnp.max(near, axis=0, keepdims=True))
    slot_peaks = [jnp.max(x, axis=0, keepdims=True) for x in listed]
    for b in range(blocks):
        for s in range(slots):
            peaks[b] = jnp.maximum(peaks[b], jnp.where(in_block[b][s], slot_peaks[s], -jnp.inf))
    row_peak = jnp.concatenate(peaks, axis=1)
    totals = by_block(jnp.sum(jnp.exp(near - row_peak), axis=0, keepdims=True))
    slot_sums = [
        jnp.sum(jnp.exp(listed[s] - of_slot(peaks, s)), axis=0, keepdims=True) for s in range(slots)
    ]
    for b in range(blocks):
        for s in range(slots):
            totals[b] = totals[b] + jnp.where(in_block[b][s], slot_sums[s], 0.0)
    log_total = row_peak + jnp.log(jnp.concatenate(totals, axis=1))
    is_positive = lax.broadcasted_iota(jnp.int32, near.shape, 0) == pos_column[...]
    positive_score = jnp.sum(jnp.where(is_positive, near, 0.0), axis=0, keepdims=True)
    losses[...] = log_total - positive_score
    grad = loss_grad[...]
    weights_in[...] = (
        grad * (jnp.exp(near - log_total) - is_positive.astype(jnp.float32))
    ).astype(jnp.bfloat16)
    logs, grads = by_block(log_total), by_block(grad)
    for s in range(slots):
        weight = jnp.where(
            info[s][2], of_slot(grads, s) * jnp.exp(listed[s] - of_slot(logs, s)), 0.0
        ).astype(jnp.bfloat16)
        weights_list[s] = weight
        q = queries[pl.ds(info[s][0] * block_size, block_size), :]
        share = (scale * dot(weight, q)).astype(jnp.bfloat16)
        for k, out in enumerate(shares):
            out[s] = share[k * shard_rows : (k + 1) * shard_rows]


def own_grads_kernel(
    lists_of, scale, table, weights_in, weights_list, queries, local, own_share, *refs
):
    pieces, (grad_queries, own_part, total) = refs[:-3], refs[-3:]
    lists = lists_of(table)
    me = lax.axis_index("dp")
    slots, block_size = weights_list.shape[0], weights_list.shape[1]
    shard_rows = own_share.shape[1]
    near = weights_in[...]
    total[...] = dot(near, local[...], TN)
    own_part[...] = scale * dot(near, queries[...])
    for s in range(slots):
        block, listed, _ = lists.slot(me, s)
        rows = jnp.concatenate([piece[s] for piece in pieces], axis=0)
        at = pl.ds(block * block_size, block_size)
        total[at, :] = total[at, :] + dot(weights_list[s], rows, TN)
        at = pl.ds(listed * shard_rows, shard_rows)
        own_part[at, :] = own_part[at, :] + own_share[s].astype(jnp.float32)
    grad_queries[...] = (scale * total[...]).astype(jnp.bfloat16)


def collect_kernel(lists_of, table, own_part, *refs):
    returned, (grad_passages, total) = refs[:-2], refs[-2:]
    lists = lists_of(table)
    me = lax.axis_index("dp")
    slots, shard_rows = returned[0].shape[0], returned[0].shape[1]
    total[...] = own_part[...]
    for k, piece in enumerate(returned):
        for s in range(slots):
            _, listed, _ = lists.slot(me ^ (k + 1), s)
            at = pl.ds(listed * shard_rows, shard_rows)
            total[at, :] = total[at, :] + piece[s].astype(jnp.float32)
    grad_passages[...] = total[...].astype(jnp.bfloat16)


def local_call(kernel, outs, scratch=(), table=True, name=None, hbm=()):
    shapes = [
        jax.ShapeDtypeStruct(*out) if i in hbm else pltpu.VMEM(*out) for i, out in enumerate(outs)
    ]

    def call(*args):
        smem = [pl.BlockSpec(memory_space=pltpu.SMEM)] if table else []
        vmem = pl.BlockSpec(memory_space=pltpu.VMEM)
        placed = [pltpu.with_memory_space_constraint(arg, pltpu.VMEM) for arg in args[len(smem) :]]
        return pl.pallas_call(
            kernel,
            out_shape=shapes,
            in_specs=smem + [vmem] * len(placed),
            out_specs=[vmem] * len(shapes),
            scratch_shapes=[pltpu.VMEM(shape, dtype) for shape, dtype in scratch],
            compiler_params=pltpu.CompilerParams(vmem_limit_bytes=KERNEL_VMEM),
            name=name,
        )(*args[: len(smem)], *placed)

    return call


def pairwise_plan(queries, passages, block_lists, list_lengths, positive, loss_grad):
    bf16, f32 = jnp.bfloat16, jnp.float32
    scale = 3.0 / math.sqrt(D)
    dp_count, me = lax.axis_size("dp"), lax.axis_index("dp")
    block_count, list_cap = block_lists.shape
    block_total, shard_rows, width = passages.shape
    block_size = shard_rows * dp_count
    query_rows = queries.shape[0]
    own_rows = block_total * shard_rows
    slots = LIVE_MAX
    peers = range(1, dp_count)
    lists_of = functools.partial(Lists, block_count=block_count, list_cap=list_cap)

    mine = jnp.concatenate([list_lengths, block_lists.reshape(-1)])
    placed = jnp.where(jnp.arange(dp_count)[:, None] == me, mine[None], 0)
    table = lax.psum(placed.reshape(-1), "dp")

    local = passages.reshape(own_rows, width)
    in_half = ((own_rows // 2, query_rows), f32)
    keep_in, send_in = local_call(
        own_scores_kernel, [in_half, in_half], table=False, name="own_scores"
    )(local, queries)

    piece = ((slots, shard_rows, width), bf16)
    outgoing = local_call(
        functools.partial(gather_kernel, lists_of, slots), [piece] * dp_count, name="gather"
    )(table, passages)
    fetched = [outgoing[0]] + [None] * (dp_count - 1)
    for k in reversed(peers):
        fetched[k] = swap(outgoing[k], "dp", k)
    in_sums = sum_over_grp(keep_in, send_in)

    list_half = ((slots // 2, block_size, block_size), f32)
    keep_list, send_list = local_call(
        functools.partial(listed_scores_kernel, lists_of), [list_half, list_half], name="listed_scores"
    )(table, queries, *fetched)
    list_sums = sum_over_grp(keep_list, send_list)

    pos_column = positive // block_size * shard_rows + positive % block_size - me * shard_rows
    losses, weights_in, weights_list, *shares = local_call(
        functools.partial(weights_kernel, lists_of, scale),
        [
            ((1, query_rows), f32),
            ((own_rows, query_rows), bf16),
            ((slots, block_size, block_size), bf16),
        ]
        + [piece] * dp_count,
        scratch=[((own_rows, query_rows), f32), ((slots, block_size, block_size), f32)],
        name="weights",
        hbm=(0,),
    )(
        table, *in_sums, *list_sums, queries,
        pos_column.reshape(1, query_rows), loss_grad.reshape(1, query_rows),
    )
    returned = [None] * dp_count
    for k in reversed(peers):
        returned[k] = swap(shares[k], "dp", k)

    grad_queries, own_part = local_call(
        functools.partial(own_grads_kernel, lists_of, scale),
        [((query_rows, width), bf16), ((own_rows, width), f32)],
        scratch=[((query_rows, width), f32)],
        hbm=(0,),
        name="own_grads",
    )(table, weights_in, weights_list, queries, local, shares[0], *fetched)
    (grad_passages,) = local_call(
        functools.partial(collect_kernel, lists_of),
        [((own_rows, width), bf16)],
        scratch=[((own_rows, width), f32)],
        hbm=(0,),
        name="collect",
    )(table, own_part, *returned[1:])
    return (
        losses.reshape(query_rows),
        grad_queries,
        grad_passages.reshape(block_total, shard_rows, width),
    )


def per_device(queries, passages, block_lists, list_lengths, positive, loss_grad):
    plan = pairwise_plan if pairwise_fits(passages.shape, block_lists.shape) else exchange_plan
    return plan(queries, passages, block_lists, list_lengths, positive, loss_grad)


def solution(mesh):
    in_specs = (P("dp", "grp"), P(None, "dp", "grp"), P("dp", None), P("dp"), P("dp"), P("dp"))
    out_specs = (P("dp"), P("dp", "grp"), P(None, "dp", "grp"))
    return jax.shard_map(
        per_device, mesh=mesh, in_specs=in_specs, out_specs=out_specs, check_vma=False
    )
```

```python
import functools
import math

import jax
import jax.numpy as jnp
from jax import lax
from jax.experimental import pallas as pl
from jax.experimental.pallas import tpu as pltpu
from jax.sharding import PartitionSpec as P


D = 4096
LIVE_MAX = 4


def pick_rows(selector, table):
    return jnp.sum(jnp.where(selector[:, :, None], table[None], 0.0), axis=1)


def exchange_plan(queries, passages, block_lists, list_lengths, positive, loss_grad):
    score_scale = 3.0 / math.sqrt(D)
    dp_count = lax.axis_size("dp")
    dp_owner = lax.axis_index("dp")
    block_count, list_cap = block_lists.shape
    block_total, shard_rows, feature_width = passages.shape
    block_size = shard_rows * dp_count
    query_rows = queries.shape[0]
    query_blocks = queries.reshape(block_count, block_size, feature_width)
    entry_index = jnp.arange(list_cap, dtype=jnp.int32)
    block_index = jnp.arange(block_count, dtype=jnp.int32)
    slot_count = LIVE_MAX
    slot_index = jnp.arange(slot_count, dtype=jnp.int32)
    list_ends = jnp.cumsum(list_lengths)
    list_starts = list_ends - list_lengths
    slot_block = jnp.minimum(
        jnp.sum((list_ends[None, :] <= slot_index[:, None]).astype(jnp.int32), axis=1),
        block_count - 1,
    )
    owner_match = slot_block[:, None] == block_index[None, :]
    offset = slot_index - jnp.sum(jnp.where(owner_match, list_starts[None, :], 0), axis=1)
    slot_live = slot_index < list_ends[block_count - 1]
    entry_match = owner_match[:, :, None] & (offset[:, None, None] == entry_index[None, None, :])
    slot_ids = jnp.sum(jnp.where(entry_match, block_lists[None], 0), axis=(1, 2))
    all_ids = lax.all_gather(slot_ids, "dp", axis=0, tiled=True)
    outgoing = passages[all_ids].reshape(dp_count, slot_count, shard_rows, feature_width)
    fetched = lax.all_to_all(outgoing, "dp", split_axis=0, concat_axis=2, tiled=True).reshape(
        slot_count, block_size, feature_width
    )
    local_rows = passages.reshape(block_total * shard_rows, feature_width)
    block_match = slot_block[:, None] == block_index[None, :]
    chosen = jnp.einsum(
        "sb,bqf->sqf",
        block_match.astype(jnp.bfloat16),
        query_blocks,
        preferred_element_type=jnp.float32,
    ).astype(jnp.bfloat16)
    part_in = lax.dot_general(
        queries, local_rows, (((1,), (1,)), ((), ())), preferred_element_type=jnp.float32
    )
    part_list = jnp.einsum("sqf,spf->sqp", chosen, fetched, preferred_element_type=jnp.float32)
    full_in, full_list = lax.psum((part_in, part_list), "grp")
    scores_in = score_scale * full_in
    scores_list = score_scale * full_list
    slot_open = block_match & slot_live[:, None]
    slot_peak = jnp.max(scores_list, axis=2)
    list_peak = jnp.max(
        jnp.where(slot_open[:, :, None], slot_peak[:, None, :], -jnp.inf), axis=0
    ).reshape(query_rows)
    row_peak = jnp.maximum(jnp.max(scores_in, axis=1), list_peak)
    slot_shift = pick_rows(block_match, row_peak.reshape(block_count, block_size))
    slot_sums = jnp.sum(jnp.exp(scores_list - slot_shift[:, :, None]), axis=2)
    list_total = jnp.sum(
        jnp.where(slot_open[:, :, None], slot_sums[:, None, :], 0.0), axis=0
    ).reshape(query_rows)
    row_total = jnp.sum(jnp.exp(scores_in - row_peak[:, None]), axis=1) + list_total
    log_total = row_peak + jnp.log(row_total)
    pos_column = positive // block_size * shard_rows + positive % block_size - dp_owner * shard_rows
    column_index = jnp.arange(block_total * shard_rows, dtype=jnp.int32)
    is_positive = column_index[None, :] == pos_column[:, None]
    positive_score = jnp.sum(jnp.where(is_positive, scores_in, 0.0), axis=1)
    losses = log_total - positive_score
    weights_in = (
        loss_grad[:, None]
        * (jnp.exp(scores_in - log_total[:, None]) - is_positive.astype(jnp.float32))
    ).astype(jnp.bfloat16)
    slot_log = pick_rows(block_match, log_total.reshape(block_count, block_size))
    slot_grad = pick_rows(block_match, loss_grad.reshape(block_count, block_size))
    weights_list = jnp.where(
        slot_live[:, None, None],
        slot_grad[:, :, None] * jnp.exp(scores_list - slot_log[:, :, None]),
        0.0,
    ).astype(jnp.bfloat16)
    near_terms = jnp.dot(weights_in, local_rows, preferred_element_type=jnp.float32)
    per_slot = jnp.einsum("sqp,spf->sqf", weights_list, fetched, preferred_element_type=jnp.float32)
    far_terms = jnp.einsum(
        "sb,sqf->bqf", block_match.astype(jnp.float32), per_slot, precision=lax.Precision.HIGHEST
    ).reshape(query_rows, feature_width)
    grad_queries = (score_scale * (near_terms + far_terms)).astype(jnp.bfloat16)
    shares = (
        score_scale
        * jnp.einsum("sqp,sqf->spf", weights_list, chosen, preferred_element_type=jnp.float32)
    ).astype(jnp.bfloat16)
    returned = lax.all_to_all(
        shares.reshape(1, slot_count, block_size, feature_width),
        "dp",
        split_axis=2,
        concat_axis=0,
        tiled=True,
    )
    own_part = score_scale * lax.dot_general(
        weights_in, queries, (((0,), (0,)), ((), ())), preferred_element_type=jnp.float32
    )
    summed = (
        own_part.reshape(block_total, shard_rows, feature_width)
        .at[all_ids]
        .add(returned.reshape(dp_count * slot_count, shard_rows, feature_width).astype(jnp.float32))
    )
    return (losses, grad_queries, summed.astype(jnp.bfloat16))


LOANS = (2, 1, 1)
KERNEL_VMEM = 8 * 1024 * 1024
NT = (((1,), (1,)), ((), ()))
TN = (((0,), (0,)), ((), ()))
NN = (((1,), (0,)), ((), ()))


def power_of_two(count):
    return count > 0 and count & (count - 1) == 0


def mirror_fits(passage_shape):
    dp_count, grp_count = lax.axis_size("dp"), lax.axis_size("grp")
    block_total, shard_rows, feature_width = passage_shape
    block_size = shard_rows * dp_count
    return (
        power_of_two(dp_count)
        and dp_count > 2
        and power_of_two(grp_count)
        and grp_count > 1
        and shard_rows % 16 == 0
        and block_size % 128 == 0
        and feature_width % 128 == 0
        and (block_total * shard_rows) % 256 == 0
        and block_total <= 4 * LIVE_MAX
        and block_total % 4 == 0
        and sum(LOANS) == LIVE_MAX
    )


def swap(value, axis, bit, takes_part=lambda i: True):
    pairs = [(i, i ^ bit) for i in range(lax.axis_size(axis)) if takes_part(i)]
    return lax.ppermute(value, axis, pairs)


def inner(i):
    half = lax.axis_size("dp") // 2
    return (i // half + i // (half // 2)) % 2 == 1


def far_rows(sources, at):
    near, far = (source[at, :] for source in sources)
    return jnp.where(inner(lax.axis_index("dp")), near, far)


def swap_shared(value, bit):
    dp_count, grp_count = lax.axis_size("dp"), lax.axis_size("grp")
    pairs = [
        (d * grp_count + g, (d ^ bit) * grp_count + (g ^ 1))
        for d in range(dp_count)
        for g in range(grp_count)
    ]
    return lax.ppermute(value, ("dp", "grp"), pairs)


def sum_over_grp(keep, send):
    half = add(keep, swap(send, "grp", 1))
    bit = 2
    while bit < lax.axis_size("grp"):
        half = add(half, swap(half, "grp", bit))
        bit *= 2
    return half, swap(half, "grp", 1)


def add_kernel(a, b, out):
    out[...] = a[...] + b[...]


def add(a, b):
    return local_call(add_kernel, [(a.shape, a.dtype)])(a, b)[0]


def join_kernel(a, b, out):
    for i in range(a.shape[0]):
        out[i] = a[i]
        out[a.shape[0] + i] = b[i]


def dot(a, b, dims=NN):
    return lax.dot_general(a, b, dims, preferred_element_type=jnp.float32)


class Lists:
    def __init__(self, table, block_count, list_cap, slots):
        self.table, self.block_count, self.list_cap = table, block_count, list_cap
        self.slots = slots

    def slot(self, side, s):
        base = side * self.block_count * (1 + self.list_cap)
        end, start, block, live = 0, 0, 0, False
        for b in range(self.block_count):
            begin = end
            end = end + self.table[base + b]
            inside = s >= begin
            block = jnp.where(inside, b, block)
            start = jnp.where(inside, begin, start)
            live = s < end
        entry = jnp.minimum(s - start, self.list_cap - 1)
        listed = self.table[base + self.block_count + block * self.list_cap + entry]
        return block, jnp.where(live, listed, 0), live

    def sides(self):
        for side in range(2):
            for s in range(self.slots):
                yield (side * self.slots + s, side, s) + self.slot(side, s)


def own_scores_kernel(local, queries, _, keep, send):
    rows = keep.shape[0]
    core = lax.axis_index("grp") & 1
    q = queries[...]
    keep[...] = dot(local[pl.ds(core * rows, rows), :], q, NT)
    send[...] = dot(local[pl.ds((1 - core) * rows, rows), :], q, NT)


def listed_rows(pieces, listed):
    rows, pieces = [], list(pieces)
    total = pieces[0].shape[0]
    while pieces:
        first, row = 0, None
        while first < total:
            piece = pieces.pop(0)
            part = piece[jnp.clip(listed - first, 0, piece.shape[0] - 1)]
            row = part if row is None else jnp.where(listed >= first, part, row)
            first += piece.shape[0]
        rows.append(row)
    return jnp.concatenate(rows, axis=0)


def listed_scores_kernel(lists_of, table, queries, *refs):
    sources, pieces, (keep, send, scores) = refs[:2], refs[2:-3], refs[-3:]
    lists = lists_of(table)
    slots, block_size = keep.shape[0], keep.shape[2]
    core = lax.axis_index("grp") & 1
    for place, side, _, block, listed, _ in lists.sides():
        at = pl.ds(block * block_size, block_size)
        rows = far_rows(sources, at) if side else queries[at, :]
        scores[place] = dot(listed_rows(pieces, listed), rows, NT)
    keep[...] = scores[pl.ds(core * slots, slots)]
    send[...] = scores[pl.ds((1 - core) * slots, slots)]


def lend_kernel(lists_of, first, table, *refs):
    pieces, loan = refs[:-1], refs[-1]
    lists = lists_of(table)
    for i in range(loan.shape[0]):
        _, listed, _ = lists.slot(1, first + i)
        loan[i] = listed_rows(pieces, listed)


def select_block(values, block):
    picked = values[0]
    for b in range(1, len(values)):
        picked = jnp.where(block == b, values[b], picked)
    return picked


def cut(row, size):
    return [row[:, i : i + size] for i in range(0, row.shape[1], size)]


def stats_kernel(
    lists_of, scale, table, in_half, in_other, list_half, list_other, per_query,
    scores_in, scores_list, stats,
):
    lists = lists_of(table)
    core = lax.axis_index("grp") & 1
    rows, slots, block_size = in_half.shape[0], lists.slots, list_half.shape[2]
    scores_in[pl.ds(core * rows, rows), :] = scale * in_half[...]
    scores_in[pl.ds((1 - core) * rows, rows), :] = scale * in_other[...]
    scores_list[pl.ds(core * slots, slots)] = scale * list_half[...]
    scores_list[pl.ds((1 - core) * slots, slots)] = scale * list_other[...]
    near = scores_in[...]
    info = list(lists.sides())
    for side in range(2):
        listed = [entry for entry in info if entry[1] == side]
        scores = [scores_list[entry[0]] for entry in listed]
        if side:
            peaks = [jnp.full((1, block_size), -jnp.inf, jnp.float32)] * lists.block_count
        else:
            peaks = cut(jnp.max(near, axis=0, keepdims=True), block_size)
        for entry, score in zip(listed, scores):
            slot_peak = jnp.max(score, axis=0, keepdims=True)
            for b in range(lists.block_count):
                counts = (entry[3] == b) & entry[5]
                peaks[b] = jnp.maximum(peaks[b], jnp.where(counts, slot_peak, -jnp.inf))
        row_peak = jnp.concatenate(peaks, axis=1)
        if side:
            totals = [jnp.zeros((1, block_size), jnp.float32)] * lists.block_count
        else:
            totals = cut(jnp.sum(jnp.exp(near - row_peak), axis=0, keepdims=True), block_size)
        for entry, score in zip(listed, scores):
            shifted = jnp.exp(score - select_block(peaks, entry[3]))
            slot_sum = jnp.sum(shifted, axis=0, keepdims=True)
            for b in range(lists.block_count):
                counts = (entry[3] == b) & entry[5]
                totals[b] = totals[b] + jnp.where(counts, slot_sum, 0.0)
        stats[2 * side : 2 * side + 1, :] = row_peak
        stats[2 * side + 1 : 2 * side + 2, :] = jnp.concatenate(totals, axis=1)
    stats[4:5, :] = per_query[0:1, :]
    stats[5:8, :] = jnp.zeros((3, stats.shape[1]), jnp.float32)


def log_sum(near, far):
    peak = jnp.maximum(near[0], far[0])
    return peak + jnp.log(near[1] * jnp.exp(near[0] - peak) + far[1] * jnp.exp(far[0] - peak))


def weights_kernel(
    lists_of, scale, table, scores_in, scores_list, stats, far_stats, per_query, queries,
    near_source, far_source, losses, weights_in, weights_own, weights_loan, *shares,
):
    lists = lists_of(table)
    block_size = scores_list.shape[2]
    shard_rows = shares[0].shape[1]
    rows = [stats[i : i + 1, :] for i in range(5)]
    mirrored = [far_stats[i : i + 1, :] for i in range(5)]
    log_total = log_sum(rows[0:2], mirrored[2:4])
    far_log = log_sum(mirrored[0:2], rows[2:4])
    grad = rows[4]
    logs = cut(log_total, block_size), cut(far_log, block_size)
    grads = cut(grad, block_size), cut(mirrored[4], block_size)
    for place, side, s, block, _, live in lists.sides():
        weight = jnp.where(
            live,
            select_block(grads[side], block)
            * jnp.exp(scores_list[place] - select_block(logs[side], block)),
            0.0,
        ).astype(jnp.bfloat16)
        (weights_loan if side else weights_own)[s] = weight
        at = pl.ds(block * block_size, block_size)
        share = scale * dot(weight, far_rows((near_source, far_source), at) if side else queries[at, :])
        share = share.astype(jnp.bfloat16)
        for k, out in enumerate(shares):
            out[place] = share[k * shard_rows : (k + 1) * shard_rows]
    near = scores_in[...]
    pos_column = per_query[1:2, :].astype(jnp.int32)
    is_positive = lax.broadcasted_iota(jnp.int32, near.shape, 0) == pos_column
    positive_score = jnp.sum(jnp.where(is_positive, near, 0.0), axis=0, keepdims=True)
    losses[...] = log_total - positive_score
    weights_in[...] = (
        grad * (jnp.exp(near - log_total) - is_positive.astype(jnp.float32))
    ).astype(jnp.bfloat16)


def own_grads_kernel(
    lists_of, scale, table, weights_in, weights_own, queries, local, own_share, *refs
):
    pieces, (query_total, own_part) = refs[:-2], refs[-2:]
    lists = lists_of(table)
    block_size, shard_rows = weights_own.shape[2], own_share.shape[1]
    near = weights_in[...]
    query_total[...] = dot(near, local[...], TN)
    own_part[...] = scale * dot(near, queries[...])
    for place, side, s, block, listed, _ in lists.sides():
        if not side:
            rows = listed_rows(pieces, listed)
            at = pl.ds(block * block_size, block_size)
            query_total[at, :] = query_total[at, :] + dot(weights_own[s], rows, TN)
        at = pl.ds(listed * shard_rows, shard_rows)
        own_part[at, :] = own_part[at, :] + own_share[place].astype(jnp.float32)


def far_grads_kernel(lists_of, scale, table, query_total, weights_far, *refs):
    loans, (grad_queries, total) = refs[:-2], refs[-2:]
    borrowed = [loan.at[i] for loan in loans for i in range(loan.shape[0])]
    lists = lists_of(table)
    block_size = weights_far.shape[2]
    total[...] = query_total[...]
    for _, side, s, block, _, _ in lists.sides():
        if not side:
            at = pl.ds(block * block_size, block_size)
            total[at, :] = total[at, :] + dot(weights_far[s], borrowed[s][...], TN)
    grad_queries[...] = (scale * total[...]).astype(jnp.bfloat16)


def collect_kernel(lists_of, own_part, *refs):
    (*inputs, grad_passages, total), count = refs, (len(refs) - 2) // 2
    tables, returned = inputs[:count], inputs[count:]
    shard_rows = returned[0].shape[1]
    total[...] = own_part[...]
    for table, piece in zip(tables, returned):
        for place, _, _, _, listed, _ in lists_of(table).sides():
            at = pl.ds(listed * shard_rows, shard_rows)
            total[at, :] = total[at, :] + piece[place].astype(jnp.float32)
    grad_passages[...] = total[...].astype(jnp.bfloat16)


def local_call(kernel, outs, scratch=(), hbm=()):
    shapes = [
        jax.ShapeDtypeStruct(*out) if i in hbm or out[1] == jnp.int32 else pltpu.VMEM(*out)
        for i, out in enumerate(outs)
    ]
    smem, vmem = (pl.BlockSpec(memory_space=space) for space in (pltpu.SMEM, pltpu.VMEM))

    def call(*args):
        tables = [arg.dtype == jnp.int32 for arg in args]
        placed = [
            arg if table else pltpu.with_memory_space_constraint(arg, pltpu.VMEM)
            for arg, table in zip(args, tables)
        ]
        return pl.pallas_call(
            kernel,
            out_shape=shapes,
            in_specs=[smem if table else vmem for table in tables],
            out_specs=[smem if out[1] == jnp.int32 else vmem for out in outs],
            scratch_shapes=[pltpu.VMEM(shape, dtype) for shape, dtype in scratch],
            compiler_params=pltpu.CompilerParams(vmem_limit_bytes=KERNEL_VMEM),
        )(*placed)

    return call


def mirror_plan(queries, passages, block_lists, list_lengths, positive, loss_grad):
    bf16, f32 = jnp.bfloat16, jnp.float32
    scale = 3.0 / math.sqrt(D)
    dp_count, me = lax.axis_size("dp"), lax.axis_index("dp")
    block_count, list_cap = block_lists.shape
    block_total, shard_rows, width = passages.shape
    block_size = shard_rows * dp_count
    query_rows = queries.shape[0]
    own_rows = block_total * shard_rows
    slots = LIVE_MAX
    half = dp_count // 2
    flip = half | half >> 1
    half_rows = half * shard_rows
    peers = range(1, half)
    lists_of = functools.partial(
        Lists, block_count=block_count, list_cap=list_cap, slots=slots
    )

    cut_at = block_total * 3 // 4
    chunks = [passages[:cut_at], passages[cut_at:]]
    by_peer = {0: [passages]}
    for k in sorted(peers, key=lambda k: (k.bit_count(), -k)):
        low = k & -k
        if k == 1:
            by_peer[k] = [swap(passages, "dp", low)]
        elif k == low:
            by_peer[k] = [swap(chunk, "dp", low) for chunk in chunks]
        else:
            by_peer[k] = [swap(chunk, "dp", low) for chunk in by_peer[k ^ low]]
    pieces = [chunk for k in range(half) for chunk in by_peer[k]]
    far_queries = (
        swap(queries, "dp", flip, inner), swap(queries, "dp", flip, lambda i: not inner(i))
    )
    mine = jnp.concatenate([list_lengths, block_lists.reshape(-1)])
    far_mine = swap(mine, "dp", flip)
    (table,) = local_call(join_kernel, [((2 * mine.shape[0],), jnp.int32)])(mine, far_mine)
    tables = [swap(table, "dp", k) for k in peers]
    pos_column = positive // block_size * shard_rows + positive % block_size - me * shard_rows
    per_query = jnp.stack([loss_grad, pos_column.astype(f32)])

    local = passages.reshape(own_rows, width)
    in_half = ((own_rows // 2, query_rows), f32)
    keep_in, send_in = local_call(own_scores_kernel, [in_half, in_half])(local, queries, per_query)
    in_sums = sum_over_grp(keep_in, send_in)

    list_half = ((slots, half_rows, block_size), f32)
    keep_list, send_list = local_call(
        functools.partial(listed_scores_kernel, lists_of),
        [list_half, list_half],
        scratch=[((2 * slots, half_rows, block_size), f32)],
    )(table, queries, *far_queries, *pieces)

    borrowed = []
    for i, count in enumerate(LOANS):
        (loan,) = local_call(
            functools.partial(lend_kernel, lists_of, sum(LOANS[:i])),
            [((count, half_rows, width), bf16)],
        )(table, *pieces)
        borrowed.append(swap(loan, "dp", flip))
    list_sums = sum_over_grp(keep_list, send_list)

    scores_in, scores_list, stats = local_call(
        functools.partial(stats_kernel, lists_of, scale),
        [
            ((own_rows, query_rows), f32),
            ((2 * slots, half_rows, block_size), f32),
            ((8, query_rows), f32),
        ],
    )(table, *in_sums, *list_sums, per_query)
    far_stats = swap_shared(stats, flip)

    weights_half = ((slots, half_rows, block_size), bf16)
    piece = ((2 * slots, shard_rows, width), bf16)
    losses, weights_in, weights_own, weights_loan, *shares = local_call(
        functools.partial(weights_kernel, lists_of, scale),
        [((1, query_rows), f32), ((own_rows, query_rows), bf16), weights_half, weights_half]
        + [piece] * half,
        hbm=(0,),
    )(table, scores_in, scores_list, stats, far_stats, per_query, queries, *far_queries)
    returned = [swap(shares[k], "dp", k) for k in reversed(peers)][::-1]
    weights_far = swap_shared(weights_loan, flip)

    query_total, own_part = local_call(
        functools.partial(own_grads_kernel, lists_of, scale),
        [((query_rows, width), f32), ((own_rows, width), f32)],
    )(table, weights_in, weights_own, queries, local, shares[0], *pieces)
    (grad_queries,) = local_call(
        functools.partial(far_grads_kernel, lists_of, scale),
        [((query_rows, width), bf16)],
        scratch=[((query_rows, width), f32)],
        hbm=(0,),
    )(table, query_total, weights_far, *borrowed)
    (grad_passages,) = local_call(
        functools.partial(collect_kernel, lists_of),
        [((own_rows, width), bf16)],
        scratch=[((own_rows, width), f32)],
        hbm=(0,),
    )(own_part, *tables, *returned)
    return (
        losses.reshape(query_rows),
        grad_queries,
        grad_passages.reshape(block_total, shard_rows, width),
    )


def per_device(queries, passages, block_lists, list_lengths, positive, loss_grad):
    plan = mirror_plan if mirror_fits(passages.shape) else exchange_plan
    return plan(queries, passages, block_lists, list_lengths, positive, loss_grad)


def solution(mesh):
    in_specs = (P("dp", "grp"), P(None, "dp", "grp"), P("dp", None), P("dp"), P("dp"), P("dp"))
    out_specs = (P("dp"), P("dp", "grp"), P(None, "dp", "grp"))
    return jax.shard_map(
        per_device, mesh=mesh, in_specs=in_specs, out_specs=out_specs, check_vma=False
    )
```

```python
import functools
import math

import jax
import jax.numpy as jnp
from jax import lax
from jax.experimental import pallas as pl
from jax.experimental.pallas import tpu as pltpu
from jax.sharding import PartitionSpec as P


D = 4096
LIVE_MAX = 4


def pick_rows(selector, table):
    return jnp.sum(jnp.where(selector[:, :, None], table[None], 0.0), axis=1)


def exchange_plan(queries, passages, block_lists, list_lengths, positive, loss_grad):
    score_scale = 3.0 / math.sqrt(D)
    dp_count = lax.axis_size("dp")
    dp_owner = lax.axis_index("dp")
    block_count, list_cap = block_lists.shape
    block_total, shard_rows, feature_width = passages.shape
    block_size = shard_rows * dp_count
    query_rows = queries.shape[0]
    query_blocks = queries.reshape(block_count, block_size, feature_width)
    entry_index = jnp.arange(list_cap, dtype=jnp.int32)
    block_index = jnp.arange(block_count, dtype=jnp.int32)
    slot_count = LIVE_MAX
    slot_index = jnp.arange(slot_count, dtype=jnp.int32)
    list_ends = jnp.cumsum(list_lengths)
    list_starts = list_ends - list_lengths
    slot_block = jnp.minimum(
        jnp.sum((list_ends[None, :] <= slot_index[:, None]).astype(jnp.int32), axis=1),
        block_count - 1,
    )
    owner_match = slot_block[:, None] == block_index[None, :]
    offset = slot_index - jnp.sum(jnp.where(owner_match, list_starts[None, :], 0), axis=1)
    slot_live = slot_index < list_ends[block_count - 1]
    entry_match = owner_match[:, :, None] & (offset[:, None, None] == entry_index[None, None, :])
    slot_ids = jnp.sum(jnp.where(entry_match, block_lists[None], 0), axis=(1, 2))
    all_ids = lax.all_gather(slot_ids, "dp", axis=0, tiled=True)
    outgoing = passages[all_ids].reshape(dp_count, slot_count, shard_rows, feature_width)
    fetched = lax.all_to_all(outgoing, "dp", split_axis=0, concat_axis=2, tiled=True).reshape(
        slot_count, block_size, feature_width
    )
    local_rows = passages.reshape(block_total * shard_rows, feature_width)
    block_match = slot_block[:, None] == block_index[None, :]
    chosen = jnp.einsum(
        "sb,bqf->sqf",
        block_match.astype(jnp.bfloat16),
        query_blocks,
        preferred_element_type=jnp.float32,
    ).astype(jnp.bfloat16)
    part_in = lax.dot_general(
        queries, local_rows, (((1,), (1,)), ((), ())), preferred_element_type=jnp.float32
    )
    part_list = jnp.einsum("sqf,spf->sqp", chosen, fetched, preferred_element_type=jnp.float32)
    full_in, full_list = lax.psum((part_in, part_list), "grp")
    scores_in = score_scale * full_in
    scores_list = score_scale * full_list
    slot_open = block_match & slot_live[:, None]
    slot_peak = jnp.max(scores_list, axis=2)
    list_peak = jnp.max(
        jnp.where(slot_open[:, :, None], slot_peak[:, None, :], -jnp.inf), axis=0
    ).reshape(query_rows)
    row_peak = jnp.maximum(jnp.max(scores_in, axis=1), list_peak)
    slot_shift = pick_rows(block_match, row_peak.reshape(block_count, block_size))
    slot_sums = jnp.sum(jnp.exp(scores_list - slot_shift[:, :, None]), axis=2)
    list_total = jnp.sum(
        jnp.where(slot_open[:, :, None], slot_sums[:, None, :], 0.0), axis=0
    ).reshape(query_rows)
    row_total = jnp.sum(jnp.exp(scores_in - row_peak[:, None]), axis=1) + list_total
    log_total = row_peak + jnp.log(row_total)
    pos_column = positive // block_size * shard_rows + positive % block_size - dp_owner * shard_rows
    column_index = jnp.arange(block_total * shard_rows, dtype=jnp.int32)
    is_positive = column_index[None, :] == pos_column[:, None]
    positive_score = jnp.sum(jnp.where(is_positive, scores_in, 0.0), axis=1)
    losses = log_total - positive_score
    weights_in = (
        loss_grad[:, None]
        * (jnp.exp(scores_in - log_total[:, None]) - is_positive.astype(jnp.float32))
    ).astype(jnp.bfloat16)
    slot_log = pick_rows(block_match, log_total.reshape(block_count, block_size))
    slot_grad = pick_rows(block_match, loss_grad.reshape(block_count, block_size))
    weights_list = jnp.where(
        slot_live[:, None, None],
        slot_grad[:, :, None] * jnp.exp(scores_list - slot_log[:, :, None]),
        0.0,
    ).astype(jnp.bfloat16)
    near_terms = jnp.dot(weights_in, local_rows, preferred_element_type=jnp.float32)
    per_slot = jnp.einsum("sqp,spf->sqf", weights_list, fetched, preferred_element_type=jnp.float32)
    far_terms = jnp.einsum(
        "sb,sqf->bqf", block_match.astype(jnp.float32), per_slot, precision=lax.Precision.HIGHEST
    ).reshape(query_rows, feature_width)
    grad_queries = (score_scale * (near_terms + far_terms)).astype(jnp.bfloat16)
    shares = (
        score_scale
        * jnp.einsum("sqp,sqf->spf", weights_list, chosen, preferred_element_type=jnp.float32)
    ).astype(jnp.bfloat16)
    returned = lax.all_to_all(
        shares.reshape(1, slot_count, block_size, feature_width),
        "dp",
        split_axis=2,
        concat_axis=0,
        tiled=True,
    )
    own_part = score_scale * lax.dot_general(
        weights_in, queries, (((0,), (0,)), ((), ())), preferred_element_type=jnp.float32
    )
    summed = (
        own_part.reshape(block_total, shard_rows, feature_width)
        .at[all_ids]
        .add(returned.reshape(dp_count * slot_count, shard_rows, feature_width).astype(jnp.float32))
    )
    return (losses, grad_queries, summed.astype(jnp.bfloat16))


KERNEL_VMEM = 8 * 1024 * 1024
NT = (((1,), (1,)), ((), ()))
TN = (((0,), (0,)), ((), ()))
NN = (((1,), (0,)), ((), ()))


def power_of_two(count):
    return count > 0 and count & (count - 1) == 0


def mirror_fits(passage_shape):
    dp_count, grp_count = lax.axis_size("dp"), lax.axis_size("grp")
    block_total, shard_rows, feature_width = passage_shape
    block_size = shard_rows * dp_count
    return (
        power_of_two(dp_count)
        and dp_count > 2
        and power_of_two(grp_count)
        and grp_count > 1
        and shard_rows % 16 == 0
        and block_size % 128 == 0
        and feature_width % 128 == 0
        and (block_total * shard_rows) % 256 == 0
        and block_total <= 4 * LIVE_MAX
        and block_total % 4 == 0
        and 2 * LIVE_MAX * shard_rows <= feature_width
        and LIVE_MAX % 2 == 0
    )


def swap(value, axis, bit, takes_part=lambda i: True):
    pairs = [(i, i ^ bit) for i in range(lax.axis_size(axis)) if takes_part(i)]
    return lax.ppermute(value, axis, pairs)


def inner(i):
    half = lax.axis_size("dp") // 2
    return (i // half + i // (half // 2)) % 2 == 1


def outer(i):
    return not inner(i)


def far_rows(sources, at):
    near, far = (source[at, :] for source in sources)
    return jnp.where(inner(lax.axis_index("dp")), near, far)


def swap_shared(value, bit):
    dp_count, grp_count = lax.axis_size("dp"), lax.axis_size("grp")
    pairs = [
        (d * grp_count + g, (d ^ bit) * grp_count + (g ^ 1))
        for d in range(dp_count)
        for g in range(grp_count)
    ]
    return lax.ppermute(value, ("dp", "grp"), pairs)


def sum_over_grp(keep, send):
    half = add(keep, swap(send, "grp", 1))
    bit = 2
    while bit < lax.axis_size("grp"):
        half = add(half, swap(half, "grp", bit))
        bit *= 2
    return half, swap(half, "grp", 1)


def add_kernel(a, b, out):
    out[...] = a[...] + b[...]


def add(a, b):
    return local_call(add_kernel, [(a.shape, a.dtype)])(a, b)[0]


def join_kernel(a, b, out):
    for i in range(a.shape[0]):
        out[i] = a[i]
        out[a.shape[0] + i] = b[i]


def dot(a, b, dims=NN):
    return lax.dot_general(a, b, dims, preferred_element_type=jnp.float32)


class Lists:
    def __init__(self, table, block_count, list_cap, slots):
        self.table, self.block_count, self.list_cap = table, block_count, list_cap
        self.slots = slots

    def slot(self, side, s):
        base = side * self.block_count * (1 + self.list_cap)
        end, start, block, live = 0, 0, 0, False
        for b in range(self.block_count):
            begin = end
            end = end + self.table[base + b]
            inside = s >= begin
            block = jnp.where(inside, b, block)
            start = jnp.where(inside, begin, start)
            live = s < end
        entry = jnp.minimum(s - start, self.list_cap - 1)
        listed = self.table[base + self.block_count + block * self.list_cap + entry]
        return block, jnp.where(live, listed, 0), live

    def sides(self):
        for side in range(2):
            for s in range(self.slots):
                yield (side * self.slots + s, side, s) + self.slot(side, s)


def own_scores_kernel(local, queries, _, keep, send):
    rows = keep.shape[0]
    core = lax.axis_index("grp") & 1
    q = queries[...]
    keep[...] = dot(local[pl.ds(core * rows, rows), :], q, NT)
    send[...] = dot(local[pl.ds((1 - core) * rows, rows), :], q, NT)


def listed_rows(pieces, listed):
    rows, pieces = [], list(pieces)
    total = pieces[0].shape[0]
    while pieces:
        first, row = 0, None
        while first < total:
            piece = pieces.pop(0)
            part = piece[jnp.clip(listed - first, 0, piece.shape[0] - 1)]
            row = part if row is None else jnp.where(listed >= first, part, row)
            first += piece.shape[0]
        rows.append(row)
    return jnp.concatenate(rows, axis=0)


def listed_scores_kernel(lists_of, table, queries, *refs):
    sources, pieces, (keep, send, scores) = refs[:2], refs[2:-3], refs[-3:]
    lists = lists_of(table)
    slots, block_size = keep.shape[0], keep.shape[2]
    core = lax.axis_index("grp") & 1
    for place, side, _, block, listed, _ in lists.sides():
        at = pl.ds(block * block_size, block_size)
        rows = far_rows(sources, at) if side else queries[at, :]
        scores[place] = dot(listed_rows(pieces, listed), rows, NT)
    keep[...] = scores[pl.ds(core * slots, slots)]
    send[...] = scores[pl.ds((1 - core) * slots, slots)]


def lend_kernel(lists_of, table, *refs):
    pieces, loan = refs[:-1], refs[-1]
    lists = lists_of(table)
    for s in range(lists.slots):
        _, listed, _ = lists.slot(1, s)
        loan[s] = listed_rows(pieces, listed)


def select_block(values, block):
    picked = values[0]
    for b in range(1, len(values)):
        picked = jnp.where(block == b, values[b], picked)
    return picked


def cut(row, size):
    return [row[:, i : i + size] for i in range(0, row.shape[1], size)]


def stats_kernel(
    lists_of, scale, table, in_half, in_other, list_half, list_other, per_query,
    scores_in, scores_list, stats,
):
    lists = lists_of(table)
    core = lax.axis_index("grp") & 1
    rows, slots, block_size = in_half.shape[0], lists.slots, list_half.shape[2]
    scores_in[pl.ds(core * rows, rows), :] = scale * in_half[...]
    scores_in[pl.ds((1 - core) * rows, rows), :] = scale * in_other[...]
    scores_list[pl.ds(core * slots, slots)] = scale * list_half[...]
    scores_list[pl.ds((1 - core) * slots, slots)] = scale * list_other[...]
    near = scores_in[...]
    info = list(lists.sides())
    for side in range(2):
        listed = [entry for entry in info if entry[1] == side]
        scores = [scores_list[entry[0]] for entry in listed]
        if side:
            peaks = [jnp.full((1, block_size), -jnp.inf, jnp.float32)] * lists.block_count
        else:
            peaks = cut(jnp.max(near, axis=0, keepdims=True), block_size)
        for entry, score in zip(listed, scores):
            slot_peak = jnp.max(score, axis=0, keepdims=True)
            for b in range(lists.block_count):
                counts = (entry[3] == b) & entry[5]
                peaks[b] = jnp.maximum(peaks[b], jnp.where(counts, slot_peak, -jnp.inf))
        row_peak = jnp.concatenate(peaks, axis=1)
        if side:
            totals = [jnp.zeros((1, block_size), jnp.float32)] * lists.block_count
        else:
            totals = cut(jnp.sum(jnp.exp(near - row_peak), axis=0, keepdims=True), block_size)
        for entry, score in zip(listed, scores):
            shifted = jnp.exp(score - select_block(peaks, entry[3]))
            slot_sum = jnp.sum(shifted, axis=0, keepdims=True)
            for b in range(lists.block_count):
                counts = (entry[3] == b) & entry[5]
                totals[b] = totals[b] + jnp.where(counts, slot_sum, 0.0)
        stats[2 * side : 2 * side + 1, :] = row_peak
        stats[2 * side + 1 : 2 * side + 2, :] = jnp.concatenate(totals, axis=1)
    stats[4:5, :] = per_query[0:1, :]
    stats[5:8, :] = jnp.zeros((3, stats.shape[1]), jnp.float32)


def log_sum(near, far):
    peak = jnp.maximum(near[0], far[0])
    return peak + jnp.log(near[1] * jnp.exp(near[0] - peak) + far[1] * jnp.exp(far[0] - peak))


def weights_kernel(
    lists_of, scale, table, scores_in, scores_list, stats, far_stats, per_query, queries,
    near_source, far_source, losses, weights_in, weights_own, weights_far, *shares,
):
    lists = lists_of(table)
    block_size = scores_list.shape[2]
    half_rows = weights_own.shape[1]
    shard_rows = half_rows // len(shares)
    rows = [stats[i : i + 1, :] for i in range(5)]
    mirrored = [far_stats[i : i + 1, :] for i in range(5)]
    log_total = log_sum(rows[0:2], mirrored[2:4])
    far_log = log_sum(mirrored[0:2], rows[2:4])
    grad = rows[4]
    logs = cut(log_total, block_size), cut(far_log, block_size)
    grads = cut(grad, block_size), cut(mirrored[4], block_size)
    for place, side, s, block, _, live in lists.sides():
        weight = jnp.where(
            live,
            select_block(grads[side], block)
            * jnp.exp(scores_list[place] - select_block(logs[side], block)),
            0.0,
        ).astype(jnp.bfloat16)
        (weights_far if side else weights_own)[s] = weight
        at = pl.ds(block * block_size, block_size)
        share = scale * dot(weight, far_rows((near_source, far_source), at) if side else queries[at, :])
        share = share.astype(jnp.bfloat16)
        for k, out in enumerate(shares):
            out[place * shard_rows : (place + 1) * shard_rows] = share[
                k * shard_rows : (k + 1) * shard_rows
            ]
    place_of = lax.broadcasted_iota(jnp.int32, (8, shares[0].shape[1]), 1) // shard_rows
    ids = jnp.zeros(place_of.shape, jnp.float32)
    for place, _, _, _, listed, _ in lists.sides():
        ids = jnp.where(place_of == place, listed.astype(jnp.float32), ids)
    for out in shares:
        out[2 * lists.slots * shard_rows :] = ids.astype(jnp.bfloat16)
    near = scores_in[...]
    pos_column = per_query[1:2, :].astype(jnp.int32)
    is_positive = lax.broadcasted_iota(jnp.int32, near.shape, 0) == pos_column
    positive_score = jnp.sum(jnp.where(is_positive, near, 0.0), axis=0, keepdims=True)
    losses[...] = log_total - positive_score
    weights_in[...] = (
        grad * (jnp.exp(near - log_total) - is_positive.astype(jnp.float32))
    ).astype(jnp.bfloat16)


def own_grads_kernel(
    lists_of, scale, table, weights_in, weights_own, queries, local, own_share, *refs
):
    pieces, (query_total, own_part) = refs[:-2], refs[-2:]
    lists = lists_of(table)
    block_size = weights_own.shape[2]
    shard_rows = (own_share.shape[0] - 8) // (2 * lists.slots)
    near = weights_in[...]
    query_total[...] = dot(near, local[...], TN)
    own_part[...] = scale * dot(near, queries[...])
    for place, side, s, block, listed, _ in lists.sides():
        if not side:
            rows = listed_rows(pieces, listed)
            at = pl.ds(block * block_size, block_size)
            query_total[at, :] = query_total[at, :] + dot(weights_own[s], rows, TN)
        at = pl.ds(listed * shard_rows, shard_rows)
        share = own_share[place * shard_rows : (place + 1) * shard_rows]
        own_part[at, :] = own_part[at, :] + share.astype(jnp.float32)


def far_grads_kernel(lists_of, scale, table, query_total, weights_far, *refs):
    near_loan, far_loan, grad_queries, total = refs
    lists = lists_of(table)
    block_size = weights_far.shape[2]
    is_inner = inner(lax.axis_index("dp"))
    total[...] = query_total[...]
    for s in range(lists.slots):
        block, _, _ = lists.slot(0, s)
        rows = jnp.where(is_inner, near_loan[s], far_loan[s])
        at = pl.ds(block * block_size, block_size)
        total[at, :] = total[at, :] + dot(weights_far[s], rows, TN)
    grad_queries[...] = (scale * total[...]).astype(jnp.bfloat16)


def collect_kernel(shard_rows, own_part, *refs):
    returned, grad_passages = refs[:-1], refs[-1]
    total = own_part[...]
    count = returned[0].shape[0] - 8
    block = lax.broadcasted_iota(jnp.int32, (total.shape[0], count), 0)
    place = lax.broadcasted_iota(jnp.int32, (total.shape[0], count), 1)
    same_row = block % shard_rows == place % shard_rows
    block = (block // shard_rows).astype(jnp.float32)
    for piece in returned:
        listed = piece[count:, :count][0:1].astype(jnp.float32)
        chosen = jnp.where(same_row & (listed == block), 1.0, 0.0).astype(jnp.bfloat16)
        total = total + dot(chosen, piece[:count])
    grad_passages[...] = total.astype(jnp.bfloat16)


def local_call(kernel, outs, scratch=(), hbm=()):
    shapes = [
        jax.ShapeDtypeStruct(*out) if i in hbm or out[1] == jnp.int32 else pltpu.VMEM(*out)
        for i, out in enumerate(outs)
    ]
    smem, vmem = (pl.BlockSpec(memory_space=space) for space in (pltpu.SMEM, pltpu.VMEM))

    def call(*args):
        tables = [arg.dtype == jnp.int32 for arg in args]
        placed = [
            arg if table else pltpu.with_memory_space_constraint(arg, pltpu.VMEM)
            for arg, table in zip(args, tables)
        ]
        return pl.pallas_call(
            kernel,
            out_shape=shapes,
            in_specs=[smem if table else vmem for table in tables],
            out_specs=[smem if out[1] == jnp.int32 else vmem for out in outs],
            scratch_shapes=[pltpu.VMEM(shape, dtype) for shape, dtype in scratch],
            compiler_params=pltpu.CompilerParams(vmem_limit_bytes=KERNEL_VMEM),
        )(*placed)

    return call


def mirror_plan(queries, passages, block_lists, list_lengths, positive, loss_grad):
    bf16, f32 = jnp.bfloat16, jnp.float32
    scale = 3.0 / math.sqrt(D)
    dp_count, me = lax.axis_size("dp"), lax.axis_index("dp")
    block_count, list_cap = block_lists.shape
    block_total, shard_rows, width = passages.shape
    block_size = shard_rows * dp_count
    query_rows = queries.shape[0]
    own_rows = block_total * shard_rows
    slots = LIVE_MAX
    half = dp_count // 2
    flip = half | half >> 1
    half_rows = half * shard_rows
    peers = range(1, half)
    lists_of = functools.partial(
        Lists, block_count=block_count, list_cap=list_cap, slots=slots
    )

    cut_at = block_total * 3 // 4
    chunks = [passages[:cut_at], passages[cut_at:]]
    by_peer = {0: [passages]}
    for k in sorted(peers, key=lambda k: (k.bit_count(), -k)):
        low = k & -k
        if k == 1:
            by_peer[k] = [swap(passages, "dp", low)]
        elif k == low:
            by_peer[k] = [swap(chunk, "dp", low) for chunk in chunks]
        else:
            by_peer[k] = [swap(chunk, "dp", low) for chunk in by_peer[k ^ low]]
    pieces = [chunk for k in range(half) for chunk in by_peer[k]]
    far_queries = (swap(queries, "dp", flip, inner), swap(queries, "dp", flip, outer))
    mine = jnp.concatenate([list_lengths, block_lists.reshape(-1)])
    far_mine = swap(mine, "dp", flip)
    (table,) = local_call(join_kernel, [((2 * mine.shape[0],), jnp.int32)])(mine, far_mine)
    pos_column = positive // block_size * shard_rows + positive % block_size - me * shard_rows
    per_query = jnp.stack([loss_grad, pos_column.astype(f32)])

    local = passages.reshape(own_rows, width)
    in_half = ((own_rows // 2, query_rows), f32)
    keep_in, send_in = local_call(own_scores_kernel, [in_half, in_half])(local, queries, per_query)
    in_sums = sum_over_grp(keep_in, send_in)

    list_half = ((slots, half_rows, block_size), f32)
    keep_list, send_list = local_call(
        functools.partial(listed_scores_kernel, lists_of),
        [list_half, list_half],
        scratch=[((2 * slots, half_rows, block_size), f32)],
    )(table, queries, *far_queries, *pieces)

    (loan,) = local_call(
        functools.partial(lend_kernel, lists_of), [((slots, half_rows, width), bf16)]
    )(table, *pieces)
    borrowed = (swap(loan, "dp", flip, inner), swap(loan, "dp", flip, outer))
    list_sums = sum_over_grp(keep_list, send_list)

    scores_in, scores_list, stats = local_call(
        functools.partial(stats_kernel, lists_of, scale),
        [
            ((own_rows, query_rows), f32),
            ((2 * slots, half_rows, block_size), f32),
            ((8, query_rows), f32),
        ],
    )(table, *in_sums, *list_sums, per_query)
    far_stats = swap_shared(stats, flip)

    weights_half = ((slots, half_rows, block_size), bf16)
    piece = ((2 * slots * shard_rows + 8, width), bf16)
    losses, weights_in, weights_own, weights_loan, *shares = local_call(
        functools.partial(weights_kernel, lists_of, scale),
        [((1, query_rows), f32), ((own_rows, query_rows), bf16), weights_half, weights_half]
        + [piece] * half,
        hbm=(0,),
    )(table, scores_in, scores_list, stats, far_stats, per_query, queries, *far_queries)
    returned = [swap(shares[k], "dp", k) for k in reversed(peers)]
    weights_far = swap(weights_loan, "dp", flip)

    query_total, own_part = local_call(
        functools.partial(own_grads_kernel, lists_of, scale),
        [((query_rows, width), f32), ((own_rows, width), f32)],
    )(table, weights_in, weights_own, queries, local, shares[0], *pieces)
    (grad_queries,) = local_call(
        functools.partial(far_grads_kernel, lists_of, scale),
        [((query_rows, width), bf16)],
        scratch=[((query_rows, width), f32)],
        hbm=(0,),
    )(table, query_total, weights_far, *borrowed)
    (grad_passages,) = local_call(
        functools.partial(collect_kernel, shard_rows), [((own_rows, width), bf16)], hbm=(0,)
    )(own_part, *returned)
    return (
        losses.reshape(query_rows),
        grad_queries,
        grad_passages.reshape(block_total, shard_rows, width),
    )


def per_device(queries, passages, block_lists, list_lengths, positive, loss_grad):
    plan = mirror_plan if mirror_fits(passages.shape) else exchange_plan
    return plan(queries, passages, block_lists, list_lengths, positive, loss_grad)


def solution(mesh):
    in_specs = (P("dp", "grp"), P(None, "dp", "grp"), P("dp", None), P("dp"), P("dp"), P("dp"))
    out_specs = (P("dp"), P("dp", "grp"), P(None, "dp", "grp"))
    return jax.shard_map(
        per_device, mesh=mesh, in_specs=in_specs, out_specs=out_specs, check_vma=False
    )
```

```python
import functools
import math

import jax
import jax.numpy as jnp
from jax import lax
from jax.experimental import pallas as pl
from jax.experimental.pallas import tpu as pltpu
from jax.sharding import PartitionSpec as P


D = 4096
LIVE_MAX = 4


def pick_rows(selector, table):
    return jnp.sum(jnp.where(selector[:, :, None], table[None], 0.0), axis=1)


def exchange_plan(queries, passages, block_lists, list_lengths, positive, loss_grad):
    score_scale = 3.0 / math.sqrt(D)
    dp_count = lax.axis_size("dp")
    dp_owner = lax.axis_index("dp")
    block_count, list_cap = block_lists.shape
    block_total, shard_rows, feature_width = passages.shape
    block_size = shard_rows * dp_count
    query_rows = queries.shape[0]
    query_blocks = queries.reshape(block_count, block_size, feature_width)
    entry_index = jnp.arange(list_cap, dtype=jnp.int32)
    block_index = jnp.arange(block_count, dtype=jnp.int32)
    slot_count = LIVE_MAX
    slot_index = jnp.arange(slot_count, dtype=jnp.int32)
    list_ends = jnp.cumsum(list_lengths)
    list_starts = list_ends - list_lengths
    slot_block = jnp.minimum(
        jnp.sum((list_ends[None, :] <= slot_index[:, None]).astype(jnp.int32), axis=1),
        block_count - 1,
    )
    owner_match = slot_block[:, None] == block_index[None, :]
    offset = slot_index - jnp.sum(jnp.where(owner_match, list_starts[None, :], 0), axis=1)
    slot_live = slot_index < list_ends[block_count - 1]
    entry_match = owner_match[:, :, None] & (offset[:, None, None] == entry_index[None, None, :])
    slot_ids = jnp.sum(jnp.where(entry_match, block_lists[None], 0), axis=(1, 2))
    all_ids = lax.all_gather(slot_ids, "dp", axis=0, tiled=True)
    outgoing = passages[all_ids].reshape(dp_count, slot_count, shard_rows, feature_width)
    fetched = lax.all_to_all(outgoing, "dp", split_axis=0, concat_axis=2, tiled=True).reshape(
        slot_count, block_size, feature_width
    )
    local_rows = passages.reshape(block_total * shard_rows, feature_width)
    block_match = slot_block[:, None] == block_index[None, :]
    chosen = jnp.einsum(
        "sb,bqf->sqf",
        block_match.astype(jnp.bfloat16),
        query_blocks,
        preferred_element_type=jnp.float32,
    ).astype(jnp.bfloat16)
    part_in = lax.dot_general(
        queries, local_rows, (((1,), (1,)), ((), ())), preferred_element_type=jnp.float32
    )
    part_list = jnp.einsum("sqf,spf->sqp", chosen, fetched, preferred_element_type=jnp.float32)
    full_in, full_list = lax.psum((part_in, part_list), "grp")
    scores_in = score_scale * full_in
    scores_list = score_scale * full_list
    slot_open = block_match & slot_live[:, None]
    slot_peak = jnp.max(scores_list, axis=2)
    list_peak = jnp.max(
        jnp.where(slot_open[:, :, None], slot_peak[:, None, :], -jnp.inf), axis=0
    ).reshape(query_rows)
    row_peak = jnp.maximum(jnp.max(scores_in, axis=1), list_peak)
    slot_shift = pick_rows(block_match, row_peak.reshape(block_count, block_size))
    slot_sums = jnp.sum(jnp.exp(scores_list - slot_shift[:, :, None]), axis=2)
    list_total = jnp.sum(
        jnp.where(slot_open[:, :, None], slot_sums[:, None, :], 0.0), axis=0
    ).reshape(query_rows)
    row_total = jnp.sum(jnp.exp(scores_in - row_peak[:, None]), axis=1) + list_total
    log_total = row_peak + jnp.log(row_total)
    pos_column = positive // block_size * shard_rows + positive % block_size - dp_owner * shard_rows
    column_index = jnp.arange(block_total * shard_rows, dtype=jnp.int32)
    is_positive = column_index[None, :] == pos_column[:, None]
    positive_score = jnp.sum(jnp.where(is_positive, scores_in, 0.0), axis=1)
    losses = log_total - positive_score
    weights_in = (
        loss_grad[:, None]
        * (jnp.exp(scores_in - log_total[:, None]) - is_positive.astype(jnp.float32))
    ).astype(jnp.bfloat16)
    slot_log = pick_rows(block_match, log_total.reshape(block_count, block_size))
    slot_grad = pick_rows(block_match, loss_grad.reshape(block_count, block_size))
    weights_list = jnp.where(
        slot_live[:, None, None],
        slot_grad[:, :, None] * jnp.exp(scores_list - slot_log[:, :, None]),
        0.0,
    ).astype(jnp.bfloat16)
    near_terms = jnp.dot(weights_in, local_rows, preferred_element_type=jnp.float32)
    per_slot = jnp.einsum("sqp,spf->sqf", weights_list, fetched, preferred_element_type=jnp.float32)
    far_terms = jnp.einsum(
        "sb,sqf->bqf", block_match.astype(jnp.float32), per_slot, precision=lax.Precision.HIGHEST
    ).reshape(query_rows, feature_width)
    grad_queries = (score_scale * (near_terms + far_terms)).astype(jnp.bfloat16)
    shares = (
        score_scale
        * jnp.einsum("sqp,sqf->spf", weights_list, chosen, preferred_element_type=jnp.float32)
    ).astype(jnp.bfloat16)
    returned = lax.all_to_all(
        shares.reshape(1, slot_count, block_size, feature_width),
        "dp",
        split_axis=2,
        concat_axis=0,
        tiled=True,
    )
    own_part = score_scale * lax.dot_general(
        weights_in, queries, (((0,), (0,)), ((), ())), preferred_element_type=jnp.float32
    )
    summed = (
        own_part.reshape(block_total, shard_rows, feature_width)
        .at[all_ids]
        .add(returned.reshape(dp_count * slot_count, shard_rows, feature_width).astype(jnp.float32))
    )
    return (losses, grad_queries, summed.astype(jnp.bfloat16))


KERNEL_VMEM = 8 * 1024 * 1024
NT = (((1,), (1,)), ((), ()))
TN = (((0,), (0,)), ((), ()))
NN = (((1,), (0,)), ((), ()))


def power_of_two(count):
    return count > 0 and count & (count - 1) == 0


def mirror_fits(passage_shape):
    dp_count, grp_count = lax.axis_size("dp"), lax.axis_size("grp")
    block_total, shard_rows, feature_width = passage_shape
    block_size = shard_rows * dp_count
    return (
        power_of_two(dp_count)
        and dp_count > 2
        and power_of_two(grp_count)
        and grp_count > 1
        and shard_rows % 16 == 0
        and block_size % 128 == 0
        and feature_width % 128 == 0
        and (block_total * shard_rows) % 256 == 0
        and block_total <= 4 * LIVE_MAX
        and block_total % 8 == 0
        and 2 * LIVE_MAX * shard_rows <= feature_width
        and LIVE_MAX % 2 == 0
    )


def swap(value, axis, bit, takes_part=lambda i: True):
    pairs = [(i, i ^ bit) for i in range(lax.axis_size(axis)) if takes_part(i)]
    return lax.ppermute(value, axis, pairs)


def inner(i):
    half = lax.axis_size("dp") // 2
    return (i // half + i // (half // 2)) % 2 == 1


def outer(i):
    return not inner(i)


def far_rows(sources, at):
    near, far = (source[at, :] for source in sources)
    return jnp.where(inner(lax.axis_index("dp")), near, far)


def swap_shared(value, bit):
    dp_count, grp_count = lax.axis_size("dp"), lax.axis_size("grp")
    pairs = [
        (d * grp_count + g, (d ^ bit) * grp_count + (g ^ 1))
        for d in range(dp_count)
        for g in range(grp_count)
    ]
    return lax.ppermute(value, ("dp", "grp"), pairs)


def sum_over_grp(keep, send):
    half = add(keep, swap(send, "grp", 1))
    bit = 2
    while bit < lax.axis_size("grp"):
        half = add(half, swap(half, "grp", bit))
        bit *= 2
    return half, swap(half, "grp", 1)


def add_kernel(a, b, out):
    out[...] = a[...] + b[...]


def add(a, b):
    return local_call(add_kernel, [(a.shape, a.dtype)])(a, b)[0]


def join_kernel(a, b, out):
    for i in range(a.shape[0]):
        out[i] = a[i]
        out[a.shape[0] + i] = b[i]


def dot(a, b, dims=NN):
    return lax.dot_general(a, b, dims, preferred_element_type=jnp.float32)


class Lists:
    def __init__(self, table, block_count, list_cap, slots):
        self.table, self.block_count, self.list_cap = table, block_count, list_cap
        self.slots = slots

    def slot(self, side, s):
        base = side * self.block_count * (1 + self.list_cap)
        end, start, block, live = 0, 0, 0, False
        for b in range(self.block_count):
            begin = end
            end = end + self.table[base + b]
            inside = s >= begin
            block = jnp.where(inside, b, block)
            start = jnp.where(inside, begin, start)
            live = s < end
        entry = jnp.minimum(s - start, self.list_cap - 1)
        listed = self.table[base + self.block_count + block * self.list_cap + entry]
        return block, jnp.where(live, listed, 0), live

    def sides(self):
        for side in range(2):
            for s in range(self.slots):
                yield (side * self.slots + s, side, s) + self.slot(side, s)


def own_scores_kernel(local, queries, _, keep, send):
    rows = keep.shape[0]
    core = lax.axis_index("grp") & 1
    q = queries[...]
    keep[...] = dot(local[pl.ds(core * rows, rows), :], q, NT)
    send[...] = dot(local[pl.ds((1 - core) * rows, rows), :], q, NT)


def listed_rows(pieces, listed):
    rows, pieces = [], list(pieces)
    total = pieces[0].shape[0]
    while pieces:
        first, row = 0, None
        while first < total:
            piece = pieces.pop(0)
            part = piece[jnp.clip(listed - first, 0, piece.shape[0] - 1)]
            row = part if row is None else jnp.where(listed >= first, part, row)
            first += piece.shape[0]
        rows.append(row)
    return jnp.concatenate(rows, axis=0)


def listed_scores_kernel(lists_of, table, queries, *refs):
    sources, pieces, (keep, send, scores) = refs[:2], refs[2:-3], refs[-3:]
    lists = lists_of(table)
    slots, block_size = keep.shape[0], keep.shape[2]
    core = lax.axis_index("grp") & 1
    for place, side, _, block, listed, _ in lists.sides():
        at = pl.ds(block * block_size, block_size)
        rows = far_rows(sources, at) if side else queries[at, :]
        scores[place] = dot(listed_rows(pieces, listed), rows, NT)
    keep[...] = scores[pl.ds(core * slots, slots)]
    send[...] = scores[pl.ds((1 - core) * slots, slots)]


def lend_kernel(lists_of, table, *refs):
    pieces, loan = refs[:-1], refs[-1]
    lists = lists_of(table)
    for s in range(lists.slots):
        _, listed, _ = lists.slot(1, s)
        loan[s] = listed_rows(pieces, listed)


def select_block(values, block):
    picked = values[0]
    for b in range(1, len(values)):
        picked = jnp.where(block == b, values[b], picked)
    return picked


def cut(row, size):
    return [row[:, i : i + size] for i in range(0, row.shape[1], size)]


def stats_kernel(
    lists_of, scale, table, in_half, in_other, list_half, list_other, per_query,
    scores_in, scores_list, stats,
):
    lists = lists_of(table)
    core = lax.axis_index("grp") & 1
    rows, slots, block_size = in_half.shape[0], lists.slots, list_half.shape[2]
    scores_in[pl.ds(core * rows, rows), :] = scale * in_half[...]
    scores_in[pl.ds((1 - core) * rows, rows), :] = scale * in_other[...]
    scores_list[pl.ds(core * slots, slots)] = scale * list_half[...]
    scores_list[pl.ds((1 - core) * slots, slots)] = scale * list_other[...]
    near = scores_in[...]
    info = list(lists.sides())
    for side in range(2):
        listed = [entry for entry in info if entry[1] == side]
        scores = [scores_list[entry[0]] for entry in listed]
        if side:
            peaks = [jnp.full((1, block_size), -jnp.inf, jnp.float32)] * lists.block_count
        else:
            peaks = cut(jnp.max(near, axis=0, keepdims=True), block_size)
        for entry, score in zip(listed, scores):
            slot_peak = jnp.max(score, axis=0, keepdims=True)
            for b in range(lists.block_count):
                counts = (entry[3] == b) & entry[5]
                peaks[b] = jnp.maximum(peaks[b], jnp.where(counts, slot_peak, -jnp.inf))
        row_peak = jnp.concatenate(peaks, axis=1)
        if side:
            totals = [jnp.zeros((1, block_size), jnp.float32)] * lists.block_count
        else:
            totals = cut(jnp.sum(jnp.exp(near - row_peak), axis=0, keepdims=True), block_size)
        for entry, score in zip(listed, scores):
            shifted = jnp.exp(score - select_block(peaks, entry[3]))
            slot_sum = jnp.sum(shifted, axis=0, keepdims=True)
            for b in range(lists.block_count):
                counts = (entry[3] == b) & entry[5]
                totals[b] = totals[b] + jnp.where(counts, slot_sum, 0.0)
        stats[2 * side : 2 * side + 1, :] = row_peak
        stats[2 * side + 1 : 2 * side + 2, :] = jnp.concatenate(totals, axis=1)
    stats[4:5, :] = per_query[0:1, :]
    stats[5:8, :] = jnp.zeros((3, stats.shape[1]), jnp.float32)


def log_sum(near, far):
    peak = jnp.maximum(near[0], far[0])
    return peak + jnp.log(near[1] * jnp.exp(near[0] - peak) + far[1] * jnp.exp(far[0] - peak))


def weights_kernel(
    lists_of, scale, table, scores_list, stats, far_stats, queries, near_source, far_source,
    weights_own, weights_far, *shares,
):
    lists = lists_of(table)
    block_size = scores_list.shape[2]
    half_rows = weights_own.shape[1]
    shard_rows = half_rows // len(shares)
    rows = [stats[i : i + 1, :] for i in range(5)]
    mirrored = [far_stats[i : i + 1, :] for i in range(5)]
    log_total = log_sum(rows[0:2], mirrored[2:4])
    far_log = log_sum(mirrored[0:2], rows[2:4])
    grad = rows[4]
    logs = cut(log_total, block_size), cut(far_log, block_size)
    grads = cut(grad, block_size), cut(mirrored[4], block_size)
    for place, side, s, block, _, live in lists.sides():
        weight = jnp.where(
            live,
            select_block(grads[side], block)
            * jnp.exp(scores_list[place] - select_block(logs[side], block)),
            0.0,
        ).astype(jnp.bfloat16)
        (weights_far if side else weights_own)[s] = weight
        at = pl.ds(block * block_size, block_size)
        share = scale * dot(weight, far_rows((near_source, far_source), at) if side else queries[at, :])
        share = share.astype(jnp.bfloat16)
        for k, out in enumerate(shares):
            out[place * shard_rows : (place + 1) * shard_rows] = share[
                k * shard_rows : (k + 1) * shard_rows
            ]
    place_of = lax.broadcasted_iota(jnp.int32, (8, shares[0].shape[1]), 1) // shard_rows
    ids = jnp.zeros(place_of.shape, jnp.float32)
    for place, _, _, _, listed, _ in lists.sides():
        ids = jnp.where(place_of == place, listed.astype(jnp.float32), ids)
    for out in shares:
        out[2 * lists.slots * shard_rows :] = ids.astype(jnp.bfloat16)


def own_grads_kernel(
    lists_of, scale, table, scores_in, stats, far_stats, per_query, weights_own, queries, local,
    own_share, *refs,
):
    pieces, (losses, query_total, own_part) = refs[:-3], refs[-3:]
    lists = lists_of(table)
    block_size = weights_own.shape[2]
    shard_rows = (own_share.shape[0] - 8) // (2 * lists.slots)
    rows = [stats[i : i + 1, :] for i in range(5)]
    log_total = log_sum(rows[0:2], [far_stats[i : i + 1, :] for i in range(2, 4)])
    scores = scores_in[...]
    pos_column = per_query[1:2, :].astype(jnp.int32)
    is_positive = lax.broadcasted_iota(jnp.int32, scores.shape, 0) == pos_column
    positive_score = jnp.sum(jnp.where(is_positive, scores, 0.0), axis=0, keepdims=True)
    losses[...] = log_total - positive_score
    near = (
        rows[4] * (jnp.exp(scores - log_total) - is_positive.astype(jnp.float32))
    ).astype(jnp.bfloat16)
    query_total[...] = dot(near, local[...], TN)
    own_part[...] = scale * dot(near, queries[...])
    for place, side, s, block, listed, _ in lists.sides():
        if not side:
            rows = listed_rows(pieces, listed)
            at = pl.ds(block * block_size, block_size)
            query_total[at, :] = query_total[at, :] + dot(weights_own[s], rows, TN)
        at = pl.ds(listed * shard_rows, shard_rows)
        share = own_share[place * shard_rows : (place + 1) * shard_rows]
        own_part[at, :] = own_part[at, :] + share.astype(jnp.float32)


def far_grads_kernel(lists_of, scale, table, query_total, weights_far, *refs):
    near_loan, far_loan, grad_queries, total = refs
    lists = lists_of(table)
    block_size = weights_far.shape[2]
    is_inner = inner(lax.axis_index("dp"))
    total[...] = query_total[...]
    for s in range(lists.slots):
        block, _, _ = lists.slot(0, s)
        rows = jnp.where(is_inner, near_loan[s], far_loan[s])
        at = pl.ds(block * block_size, block_size)
        total[at, :] = total[at, :] + dot(weights_far[s], rows, TN)
    grad_queries[...] = (scale * total[...]).astype(jnp.bfloat16)


def collect_kernel(shard_rows, own_part, *refs):
    returned, grad_passages = refs[:-1], refs[-1]
    total = own_part[...]
    count = returned[0].shape[0] - 8
    block = lax.broadcasted_iota(jnp.int32, (total.shape[0], count), 0)
    place = lax.broadcasted_iota(jnp.int32, (total.shape[0], count), 1)
    same_row = block % shard_rows == place % shard_rows
    block = (block // shard_rows).astype(jnp.float32)
    for piece in returned:
        listed = piece[count:, :count][0:1].astype(jnp.float32)
        chosen = jnp.where(same_row & (listed == block), 1.0, 0.0).astype(jnp.bfloat16)
        total = total + dot(chosen, piece[:count])
    grad_passages[...] = total.astype(jnp.bfloat16)


def local_call(kernel, outs, scratch=(), hbm=()):
    shapes = [
        jax.ShapeDtypeStruct(*out) if i in hbm or out[1] == jnp.int32 else pltpu.VMEM(*out)
        for i, out in enumerate(outs)
    ]
    smem, vmem = (pl.BlockSpec(memory_space=space) for space in (pltpu.SMEM, pltpu.VMEM))

    def call(*args):
        tables = [arg.dtype == jnp.int32 for arg in args]
        placed = [
            arg if table else pltpu.with_memory_space_constraint(arg, pltpu.VMEM)
            for arg, table in zip(args, tables)
        ]
        return pl.pallas_call(
            kernel,
            out_shape=shapes,
            in_specs=[smem if table else vmem for table in tables],
            out_specs=[smem if out[1] == jnp.int32 else vmem for out in outs],
            scratch_shapes=[pltpu.VMEM(shape, dtype) for shape, dtype in scratch],
            compiler_params=pltpu.CompilerParams(vmem_limit_bytes=KERNEL_VMEM),
        )(*placed)

    return call


def mirror_plan(queries, passages, block_lists, list_lengths, positive, loss_grad):
    bf16, f32 = jnp.bfloat16, jnp.float32
    scale = 3.0 / math.sqrt(D)
    dp_count, me = lax.axis_size("dp"), lax.axis_index("dp")
    block_count, list_cap = block_lists.shape
    block_total, shard_rows, width = passages.shape
    block_size = shard_rows * dp_count
    query_rows = queries.shape[0]
    own_rows = block_total * shard_rows
    slots = LIVE_MAX
    half = dp_count // 2
    flip = half | half >> 1
    half_rows = half * shard_rows
    peers = range(1, half)
    lists_of = functools.partial(
        Lists, block_count=block_count, list_cap=list_cap, slots=slots
    )

    cut_at = block_total * 5 // 8
    chunks = [passages[:cut_at], passages[cut_at:]]
    by_peer = {0: [passages]}
    for k in sorted(peers, key=lambda k: (k.bit_count(), -k)):
        low = k & -k
        if k == 1:
            by_peer[k] = [swap(passages, "dp", low)]
        elif k == low:
            by_peer[k] = [swap(chunk, "dp", low) for chunk in chunks]
        else:
            by_peer[k] = [swap(chunk, "dp", low) for chunk in by_peer[k ^ low]]
    pieces = [chunk for k in range(half) for chunk in by_peer[k]]
    far_queries = (swap(queries, "dp", flip, inner), swap(queries, "dp", flip, outer))
    mine = jnp.concatenate([list_lengths, block_lists.reshape(-1)])
    far_mine = swap(mine, "dp", flip)
    (table,) = local_call(join_kernel, [((2 * mine.shape[0],), jnp.int32)])(mine, far_mine)
    pos_column = positive // block_size * shard_rows + positive % block_size - me * shard_rows
    per_query = jnp.stack([loss_grad, pos_column.astype(f32)])

    local = passages.reshape(own_rows, width)
    in_half = ((own_rows // 2, query_rows), f32)
    keep_in, send_in = local_call(own_scores_kernel, [in_half, in_half])(local, queries, per_query)
    in_sums = sum_over_grp(keep_in, send_in)

    list_half = ((slots, half_rows, block_size), f32)
    keep_list, send_list = local_call(
        functools.partial(listed_scores_kernel, lists_of),
        [list_half, list_half],
        scratch=[((2 * slots, half_rows, block_size), f32)],
    )(table, queries, *far_queries, *pieces)

    (loan,) = local_call(
        functools.partial(lend_kernel, lists_of), [((slots, half_rows, width), bf16)]
    )(table, *pieces)
    borrowed = (swap(loan, "dp", flip, inner), swap(loan, "dp", flip, outer))
    list_sums = sum_over_grp(keep_list, send_list)

    scores_in, scores_list, stats = local_call(
        functools.partial(stats_kernel, lists_of, scale),
        [
            ((own_rows, query_rows), f32),
            ((2 * slots, half_rows, block_size), f32),
            ((8, query_rows), f32),
        ],
    )(table, *in_sums, *list_sums, per_query)
    far_stats = swap_shared(stats, flip)

    weights_half = ((slots, half_rows, block_size), bf16)
    piece = ((2 * slots * shard_rows + 8, width), bf16)
    weights_own, weights_loan, *shares = local_call(
        functools.partial(weights_kernel, lists_of, scale),
        [weights_half, weights_half] + [piece] * half,
    )(table, scores_list, stats, far_stats, queries, *far_queries)
    returned = [swap(shares[k], "dp", k) for k in reversed(peers)]
    weights_far = swap(weights_loan, "dp", flip)

    losses, query_total, own_part = local_call(
        functools.partial(own_grads_kernel, lists_of, scale),
        [((1, query_rows), f32), ((query_rows, width), f32), ((own_rows, width), f32)],
        hbm=(0,),
    )(
        table, scores_in, stats, far_stats, per_query, weights_own, queries, local, shares[0],
        *pieces,
    )
    (grad_queries,) = local_call(
        functools.partial(far_grads_kernel, lists_of, scale),
        [((query_rows, width), bf16)],
        scratch=[((query_rows, width), f32)],
        hbm=(0,),
    )(table, query_total, weights_far, *borrowed)
    (grad_passages,) = local_call(
        functools.partial(collect_kernel, shard_rows), [((own_rows, width), bf16)], hbm=(0,)
    )(own_part, *returned)
    return (
        losses.reshape(query_rows),
        grad_queries,
        grad_passages.reshape(block_total, shard_rows, width),
    )


def per_device(queries, passages, block_lists, list_lengths, positive, loss_grad):
    plan = mirror_plan if mirror_fits(passages.shape) else exchange_plan
    return plan(queries, passages, block_lists, list_lengths, positive, loss_grad)


def solution(mesh):
    in_specs = (P("dp", "grp"), P(None, "dp", "grp"), P("dp", None), P("dp"), P("dp"), P("dp"))
    out_specs = (P("dp"), P("dp", "grp"), P(None, "dp", "grp"))
    return jax.shard_map(
        per_device, mesh=mesh, in_specs=in_specs, out_specs=out_specs, check_vma=False
    )
```

```python
import functools
import math

import jax
import jax.numpy as jnp
from jax import lax
from jax.experimental import pallas as pl
from jax.experimental.pallas import tpu as pltpu
from jax.sharding import PartitionSpec as P


D = 4096
LIVE_MAX = 4


def pick_rows(selector, table):
    return jnp.sum(jnp.where(selector[:, :, None], table[None], 0.0), axis=1)


def exchange_plan(queries, passages, block_lists, list_lengths, positive, loss_grad):
    score_scale = 3.0 / math.sqrt(D)
    dp_count = lax.axis_size("dp")
    dp_owner = lax.axis_index("dp")
    block_count, list_cap = block_lists.shape
    block_total, shard_rows, feature_width = passages.shape
    block_size = shard_rows * dp_count
    query_rows = queries.shape[0]
    query_blocks = queries.reshape(block_count, block_size, feature_width)
    entry_index = jnp.arange(list_cap, dtype=jnp.int32)
    block_index = jnp.arange(block_count, dtype=jnp.int32)
    slot_count = LIVE_MAX
    slot_index = jnp.arange(slot_count, dtype=jnp.int32)
    list_ends = jnp.cumsum(list_lengths)
    list_starts = list_ends - list_lengths
    slot_block = jnp.minimum(
        jnp.sum((list_ends[None, :] <= slot_index[:, None]).astype(jnp.int32), axis=1),
        block_count - 1,
    )
    owner_match = slot_block[:, None] == block_index[None, :]
    offset = slot_index - jnp.sum(jnp.where(owner_match, list_starts[None, :], 0), axis=1)
    slot_live = slot_index < list_ends[block_count - 1]
    entry_match = owner_match[:, :, None] & (offset[:, None, None] == entry_index[None, None, :])
    slot_ids = jnp.sum(jnp.where(entry_match, block_lists[None], 0), axis=(1, 2))
    all_ids = lax.all_gather(slot_ids, "dp", axis=0, tiled=True)
    outgoing = passages[all_ids].reshape(dp_count, slot_count, shard_rows, feature_width)
    fetched = lax.all_to_all(outgoing, "dp", split_axis=0, concat_axis=2, tiled=True).reshape(
        slot_count, block_size, feature_width
    )
    local_rows = passages.reshape(block_total * shard_rows, feature_width)
    block_match = slot_block[:, None] == block_index[None, :]
    chosen = jnp.einsum(
        "sb,bqf->sqf",
        block_match.astype(jnp.bfloat16),
        query_blocks,
        preferred_element_type=jnp.float32,
    ).astype(jnp.bfloat16)
    part_in = lax.dot_general(
        queries, local_rows, (((1,), (1,)), ((), ())), preferred_element_type=jnp.float32
    )
    part_list = jnp.einsum("sqf,spf->sqp", chosen, fetched, preferred_element_type=jnp.float32)
    full_in, full_list = lax.psum((part_in, part_list), "grp")
    scores_in = score_scale * full_in
    scores_list = score_scale * full_list
    slot_open = block_match & slot_live[:, None]
    slot_peak = jnp.max(scores_list, axis=2)
    list_peak = jnp.max(
        jnp.where(slot_open[:, :, None], slot_peak[:, None, :], -jnp.inf), axis=0
    ).reshape(query_rows)
    row_peak = jnp.maximum(jnp.max(scores_in, axis=1), list_peak)
    slot_shift = pick_rows(block_match, row_peak.reshape(block_count, block_size))
    slot_sums = jnp.sum(jnp.exp(scores_list - slot_shift[:, :, None]), axis=2)
    list_total = jnp.sum(
        jnp.where(slot_open[:, :, None], slot_sums[:, None, :], 0.0), axis=0
    ).reshape(query_rows)
    row_total = jnp.sum(jnp.exp(scores_in - row_peak[:, None]), axis=1) + list_total
    log_total = row_peak + jnp.log(row_total)
    pos_column = positive // block_size * shard_rows + positive % block_size - dp_owner * shard_rows
    column_index = jnp.arange(block_total * shard_rows, dtype=jnp.int32)
    is_positive = column_index[None, :] == pos_column[:, None]
    positive_score = jnp.sum(jnp.where(is_positive, scores_in, 0.0), axis=1)
    losses = log_total - positive_score
    weights_in = (
        loss_grad[:, None]
        * (jnp.exp(scores_in - log_total[:, None]) - is_positive.astype(jnp.float32))
    ).astype(jnp.bfloat16)
    slot_log = pick_rows(block_match, log_total.reshape(block_count, block_size))
    slot_grad = pick_rows(block_match, loss_grad.reshape(block_count, block_size))
    weights_list = jnp.where(
        slot_live[:, None, None],
        slot_grad[:, :, None] * jnp.exp(scores_list - slot_log[:, :, None]),
        0.0,
    ).astype(jnp.bfloat16)
    near_terms = jnp.dot(weights_in, local_rows, preferred_element_type=jnp.float32)
    per_slot = jnp.einsum("sqp,spf->sqf", weights_list, fetched, preferred_element_type=jnp.float32)
    far_terms = jnp.einsum(
        "sb,sqf->bqf", block_match.astype(jnp.float32), per_slot, precision=lax.Precision.HIGHEST
    ).reshape(query_rows, feature_width)
    grad_queries = (score_scale * (near_terms + far_terms)).astype(jnp.bfloat16)
    shares = (
        score_scale
        * jnp.einsum("sqp,sqf->spf", weights_list, chosen, preferred_element_type=jnp.float32)
    ).astype(jnp.bfloat16)
    returned = lax.all_to_all(
        shares.reshape(1, slot_count, block_size, feature_width),
        "dp",
        split_axis=2,
        concat_axis=0,
        tiled=True,
    )
    own_part = score_scale * lax.dot_general(
        weights_in, queries, (((0,), (0,)), ((), ())), preferred_element_type=jnp.float32
    )
    summed = (
        own_part.reshape(block_total, shard_rows, feature_width)
        .at[all_ids]
        .add(returned.reshape(dp_count * slot_count, shard_rows, feature_width).astype(jnp.float32))
    )
    return (losses, grad_queries, summed.astype(jnp.bfloat16))


KERNEL_VMEM = 8 * 1024 * 1024
NT = (((1,), (1,)), ((), ()))
TN = (((0,), (0,)), ((), ()))
NN = (((1,), (0,)), ((), ()))


def power_of_two(count):
    return count > 0 and count & (count - 1) == 0


def mirror_fits(passage_shape):
    dp_count, grp_count = lax.axis_size("dp"), lax.axis_size("grp")
    block_total, shard_rows, feature_width = passage_shape
    block_size = shard_rows * dp_count
    return (
        power_of_two(dp_count)
        and dp_count > 2
        and power_of_two(grp_count)
        and grp_count > 1
        and shard_rows % 16 == 0
        and block_size % 128 == 0
        and feature_width % 128 == 0
        and (block_total * shard_rows) % 256 == 0
        and block_total <= 4 * LIVE_MAX
        and block_total % 16 == 0
        and 2 * LIVE_MAX * shard_rows <= feature_width
        and dp_count > 4
        and LIVE_MAX % 2 == 0
    )


def swap(value, axis, bit, takes_part=lambda i: True):
    pairs = [(i, i ^ bit) for i in range(lax.axis_size(axis)) if takes_part(i)]
    return lax.ppermute(value, axis, pairs)


def inner(i):
    half = lax.axis_size("dp") // 2
    return (i // half + i // (half // 2)) % 2 == 1


def outer(i):
    return not inner(i)


def far_rows(sources, at):
    near, far = (source[at, :] for source in sources)
    return jnp.where(inner(lax.axis_index("dp")), near, far)


def swap_shared(value, bit):
    dp_count, grp_count = lax.axis_size("dp"), lax.axis_size("grp")
    pairs = [
        (d * grp_count + g, (d ^ bit) * grp_count + (g ^ 1))
        for d in range(dp_count)
        for g in range(grp_count)
    ]
    return lax.ppermute(value, ("dp", "grp"), pairs)


def sum_over_grp(keep, send):
    half = add(keep, swap(send, "grp", 1))
    bit = 2
    while bit < lax.axis_size("grp"):
        half = add(half, swap(half, "grp", bit))
        bit *= 2
    return half, swap(half, "grp", 1)


def add_kernel(a, b, out):
    out[...] = a[...] + b[...]


def add(a, b):
    return local_call(add_kernel, [(a.shape, a.dtype)])(a, b)[0]


def join_kernel(a, b, out):
    for i in range(a.shape[0]):
        out[i] = a[i]
        out[a.shape[0] + i] = b[i]


def dot(a, b, dims=NN):
    return lax.dot_general(a, b, dims, preferred_element_type=jnp.float32)


class Lists:
    def __init__(self, table, block_count, list_cap, slots):
        self.table, self.block_count, self.list_cap = table, block_count, list_cap
        self.slots = slots

    def slot(self, side, s):
        base = side * self.block_count * (1 + self.list_cap)
        end, start, block, live = 0, 0, 0, False
        for b in range(self.block_count):
            begin = end
            end = end + self.table[base + b]
            inside = s >= begin
            block = jnp.where(inside, b, block)
            start = jnp.where(inside, begin, start)
            live = s < end
        entry = jnp.minimum(s - start, self.list_cap - 1)
        listed = self.table[base + self.block_count + block * self.list_cap + entry]
        return block, jnp.where(live, listed, 0), live

    def sides(self):
        for side in range(2):
            for s in range(self.slots):
                yield (side * self.slots + s, side, s) + self.slot(side, s)


def cut_kernel(rows, *chunks):
    first = 0
    for chunk in chunks:
        chunk[...] = rows[first : first + chunk.shape[0]]
        first += chunk.shape[0]


def own_scores_kernel(local, queries, _, keep, send):
    rows = keep.shape[0]
    core = lax.axis_index("grp") & 1
    q = queries[...]
    keep[...] = dot(local[pl.ds(core * rows, rows), :], q, NT)
    send[...] = dot(local[pl.ds((1 - core) * rows, rows), :], q, NT)


def listed_rows(pieces, listed):
    rows, pieces = [], list(pieces)
    total = pieces[0].shape[0]
    while pieces:
        first, row = 0, None
        while first < total:
            piece = pieces.pop(0)
            part = piece[jnp.clip(listed - first, 0, piece.shape[0] - 1)]
            row = part if row is None else jnp.where(listed >= first, part, row)
            first += piece.shape[0]
        rows.append(row)
    return jnp.concatenate(rows, axis=0)


def listed_scores_kernel(lists_of, table, queries, *refs):
    sources, pieces, (keep, send, scores) = refs[:2], refs[2:-3], refs[-3:]
    lists = lists_of(table)
    slots, block_size = keep.shape[0], keep.shape[2]
    core = lax.axis_index("grp") & 1
    for place, side, _, block, listed, _ in lists.sides():
        at = pl.ds(block * block_size, block_size)
        rows = far_rows(sources, at) if side else queries[at, :]
        scores[place] = dot(listed_rows(pieces, listed), rows, NT)
    keep[...] = scores[pl.ds(core * slots, slots)]
    send[...] = scores[pl.ds((1 - core) * slots, slots)]


def lend_kernel(lists_of, table, *refs):
    pieces, loan = refs[:-1], refs[-1]
    lists = lists_of(table)
    for s in range(lists.slots):
        _, listed, _ = lists.slot(1, s)
        loan[s] = listed_rows(pieces, listed)


def select_block(values, block):
    picked = values[0]
    for b in range(1, len(values)):
        picked = jnp.where(block == b, values[b], picked)
    return picked


def cut(row, size):
    return [row[:, i : i + size] for i in range(0, row.shape[1], size)]


def stats_kernel(
    lists_of, scale, table, in_half, in_other, list_half, list_other, per_query,
    scores_in, scores_list, stats,
):
    lists = lists_of(table)
    core = lax.axis_index("grp") & 1
    rows, slots, block_size = in_half.shape[0], lists.slots, list_half.shape[2]
    scores_in[pl.ds(core * rows, rows), :] = scale * in_half[...]
    scores_in[pl.ds((1 - core) * rows, rows), :] = scale * in_other[...]
    scores_list[pl.ds(core * slots, slots)] = scale * list_half[...]
    scores_list[pl.ds((1 - core) * slots, slots)] = scale * list_other[...]
    near = scores_in[...]
    info = list(lists.sides())
    for side in range(2):
        listed = [entry for entry in info if entry[1] == side]
        scores = [scores_list[entry[0]] for entry in listed]
        if side:
            peaks = [jnp.full((1, block_size), -jnp.inf, jnp.float32)] * lists.block_count
        else:
            peaks = cut(jnp.max(near, axis=0, keepdims=True), block_size)
        for entry, score in zip(listed, scores):
            slot_peak = jnp.max(score, axis=0, keepdims=True)
            for b in range(lists.block_count):
                counts = (entry[3] == b) & entry[5]
                peaks[b] = jnp.maximum(peaks[b], jnp.where(counts, slot_peak, -jnp.inf))
        row_peak = jnp.concatenate(peaks, axis=1)
        if side:
            totals = [jnp.zeros((1, block_size), jnp.float32)] * lists.block_count
        else:
            totals = cut(jnp.sum(jnp.exp(near - row_peak), axis=0, keepdims=True), block_size)
        for entry, score in zip(listed, scores):
            shifted = jnp.exp(score - select_block(peaks, entry[3]))
            slot_sum = jnp.sum(shifted, axis=0, keepdims=True)
            for b in range(lists.block_count):
                counts = (entry[3] == b) & entry[5]
                totals[b] = totals[b] + jnp.where(counts, slot_sum, 0.0)
        stats[2 * side : 2 * side + 1, :] = row_peak
        stats[2 * side + 1 : 2 * side + 2, :] = jnp.concatenate(totals, axis=1)
    stats[4:5, :] = per_query[0:1, :]
    stats[5:8, :] = jnp.zeros((3, stats.shape[1]), jnp.float32)


def log_sum(near, far):
    peak = jnp.maximum(near[0], far[0])
    return peak + jnp.log(near[1] * jnp.exp(near[0] - peak) + far[1] * jnp.exp(far[0] - peak))


def weights_kernel(
    lists_of, scale, table, scores_list, stats, far_stats, queries, near_source, far_source,
    weights_own, weights_far, *shares,
):
    lists = lists_of(table)
    block_size = scores_list.shape[2]
    half_rows = weights_own.shape[1]
    shard_rows = half_rows // len(shares)
    rows = [stats[i : i + 1, :] for i in range(5)]
    mirrored = [far_stats[i : i + 1, :] for i in range(5)]
    log_total = log_sum(rows[0:2], mirrored[2:4])
    far_log = log_sum(mirrored[0:2], rows[2:4])
    grad = rows[4]
    logs = cut(log_total, block_size), cut(far_log, block_size)
    grads = cut(grad, block_size), cut(mirrored[4], block_size)
    for place, side, s, block, _, live in lists.sides():
        weight = jnp.where(
            live,
            select_block(grads[side], block)
            * jnp.exp(scores_list[place] - select_block(logs[side], block)),
            0.0,
        ).astype(jnp.bfloat16)
        (weights_far if side else weights_own)[s] = weight
        at = pl.ds(block * block_size, block_size)
        share = scale * dot(weight, far_rows((near_source, far_source), at) if side else queries[at, :])
        share = share.astype(jnp.bfloat16)
        for k, out in enumerate(shares):
            out[place * shard_rows : (place + 1) * shard_rows] = share[
                k * shard_rows : (k + 1) * shard_rows
            ]
    place_of = lax.broadcasted_iota(jnp.int32, (8, shares[0].shape[1]), 1) // shard_rows
    ids = jnp.zeros(place_of.shape, jnp.float32)
    for place, _, _, _, listed, _ in lists.sides():
        ids = jnp.where(place_of == place, listed.astype(jnp.float32), ids)
    for out in shares:
        out[2 * lists.slots * shard_rows :] = ids.astype(jnp.bfloat16)


def own_grads_kernel(
    lists_of, scale, table, scores_in, stats, far_stats, per_query, weights_own, queries, local,
    own_share, *refs,
):
    pieces, (losses, query_total, own_part) = refs[:-3], refs[-3:]
    lists = lists_of(table)
    block_size = weights_own.shape[2]
    shard_rows = (own_share.shape[0] - 8) // (2 * lists.slots)
    rows = [stats[i : i + 1, :] for i in range(5)]
    log_total = log_sum(rows[0:2], [far_stats[i : i + 1, :] for i in range(2, 4)])
    scores = scores_in[...]
    pos_column = per_query[1:2, :].astype(jnp.int32)
    is_positive = lax.broadcasted_iota(jnp.int32, scores.shape, 0) == pos_column
    positive_score = jnp.sum(jnp.where(is_positive, scores, 0.0), axis=0, keepdims=True)
    losses[...] = log_total - positive_score
    near = (
        rows[4] * (jnp.exp(scores - log_total) - is_positive.astype(jnp.float32))
    ).astype(jnp.bfloat16)
    query_total[...] = dot(near, local[...], TN)
    own_part[...] = scale * dot(near, queries[...])
    for place, side, s, block, listed, _ in lists.sides():
        if not side:
            rows = listed_rows(pieces, listed)
            at = pl.ds(block * block_size, block_size)
            query_total[at, :] = query_total[at, :] + dot(weights_own[s], rows, TN)
        at = pl.ds(listed * shard_rows, shard_rows)
        share = own_share[place * shard_rows : (place + 1) * shard_rows]
        own_part[at, :] = own_part[at, :] + share.astype(jnp.float32)


def far_grads_kernel(lists_of, scale, table, query_total, weights_far, *refs):
    near_loan, far_loan, grad_queries, total = refs
    lists = lists_of(table)
    block_size = weights_far.shape[2]
    is_inner = inner(lax.axis_index("dp"))
    total[...] = query_total[...]
    for s in range(lists.slots):
        block, _, _ = lists.slot(0, s)
        rows = jnp.where(is_inner, near_loan[s], far_loan[s])
        at = pl.ds(block * block_size, block_size)
        total[at, :] = total[at, :] + dot(weights_far[s], rows, TN)
    grad_queries[...] = (scale * total[...]).astype(jnp.bfloat16)


def collect_kernel(shard_rows, own_part, *refs):
    returned, grad_passages = refs[:-1], refs[-1]
    total = own_part[...]
    count = returned[0].shape[0] - 8
    block = lax.broadcasted_iota(jnp.int32, (total.shape[0], count), 0)
    place = lax.broadcasted_iota(jnp.int32, (total.shape[0], count), 1)
    same_row = block % shard_rows == place % shard_rows
    block = (block // shard_rows).astype(jnp.float32)
    for piece in returned:
        listed = piece[count:, :count][0:1].astype(jnp.float32)
        chosen = jnp.where(same_row & (listed == block), 1.0, 0.0).astype(jnp.bfloat16)
        total = total + dot(chosen, piece[:count])
    grad_passages[...] = total.astype(grad_passages.dtype)


def local_call(kernel, outs, scratch=(), hbm=()):
    shapes = [
        jax.ShapeDtypeStruct(*out) if i in hbm or out[1] == jnp.int32 else pltpu.VMEM(*out)
        for i, out in enumerate(outs)
    ]
    smem, vmem = (pl.BlockSpec(memory_space=space) for space in (pltpu.SMEM, pltpu.VMEM))

    def call(*args):
        tables = [arg.dtype == jnp.int32 for arg in args]
        placed = [
            arg if table else pltpu.with_memory_space_constraint(arg, pltpu.VMEM)
            for arg, table in zip(args, tables)
        ]
        return pl.pallas_call(
            kernel,
            out_shape=shapes,
            in_specs=[smem if table else vmem for table in tables],
            out_specs=[smem if out[1] == jnp.int32 else vmem for out in outs],
            scratch_shapes=[pltpu.VMEM(shape, dtype) for shape, dtype in scratch],
            compiler_params=pltpu.CompilerParams(vmem_limit_bytes=KERNEL_VMEM),
        )(*placed)

    return call


def mirror_plan(queries, passages, block_lists, list_lengths, positive, loss_grad):
    bf16, f32 = jnp.bfloat16, jnp.float32
    scale = 3.0 / math.sqrt(D)
    dp_count, me = lax.axis_size("dp"), lax.axis_index("dp")
    block_count, list_cap = block_lists.shape
    block_total, shard_rows, width = passages.shape
    block_size = shard_rows * dp_count
    query_rows = queries.shape[0]
    own_rows = block_total * shard_rows
    slots = LIVE_MAX
    half = dp_count // 2
    flip = half | half >> 1
    half_rows = half * shard_rows
    peers = range(1, half)
    lists_of = functools.partial(
        Lists, block_count=block_count, list_cap=list_cap, slots=slots
    )

    cut_at = block_total * 11 // 16
    chunks = local_call(
        cut_kernel, [((n, shard_rows, width), bf16) for n in (cut_at, block_total - cut_at)]
    )(passages)
    by_peer = {0: [passages]}
    for k in sorted(peers, key=lambda k: (k.bit_count(), -k)):
        low = k & -k
        if k == 1:
            by_peer[k] = [swap(passages, "dp", low)]
        elif k == low:
            by_peer[k] = [swap(chunk, "dp", low) for chunk in chunks]
        else:
            by_peer[k] = [swap(chunk, "dp", low) for chunk in by_peer[k ^ low]]
    pieces = [chunk for k in range(half) for chunk in by_peer[k]]
    far_queries = (swap(queries, "dp", flip, inner), swap(queries, "dp", flip, outer))
    mine = jnp.concatenate([list_lengths, block_lists.reshape(-1)])
    far_mine = swap(mine, "dp", flip)
    (table,) = local_call(join_kernel, [((2 * mine.shape[0],), jnp.int32)])(mine, far_mine)
    pos_column = positive // block_size * shard_rows + positive % block_size - me * shard_rows
    per_query = jnp.stack([loss_grad, pos_column.astype(f32)])

    local = passages.reshape(own_rows, width)
    in_half = ((own_rows // 2, query_rows), f32)
    keep_in, send_in = local_call(own_scores_kernel, [in_half, in_half])(local, queries, per_query)
    in_sums = sum_over_grp(keep_in, send_in)

    list_half = ((slots, half_rows, block_size), f32)
    keep_list, send_list = local_call(
        functools.partial(listed_scores_kernel, lists_of),
        [list_half, list_half],
        scratch=[((2 * slots, half_rows, block_size), f32)],
    )(table, queries, *far_queries, *pieces)

    (loan,) = local_call(
        functools.partial(lend_kernel, lists_of), [((slots, half_rows, width), bf16)]
    )(table, *pieces)
    borrowed = (swap(loan, "dp", flip, inner), swap(loan, "dp", flip, outer))
    list_sums = sum_over_grp(keep_list, send_list)

    scores_in, scores_list, stats = local_call(
        functools.partial(stats_kernel, lists_of, scale),
        [
            ((own_rows, query_rows), f32),
            ((2 * slots, half_rows, block_size), f32),
            ((8, query_rows), f32),
        ],
    )(table, *in_sums, *list_sums, per_query)
    far_stats = swap_shared(stats, flip)

    weights_half = ((slots, half_rows, block_size), bf16)
    piece = ((2 * slots * shard_rows + 8, width), bf16)
    weights_own, weights_loan, *shares = local_call(
        functools.partial(weights_kernel, lists_of, scale),
        [weights_half, weights_half] + [piece] * half,
    )(table, scores_list, stats, far_stats, queries, *far_queries)
    returned = [swap(shares[k], "dp", k) for k in reversed(peers)]
    weights_far = swap(weights_loan, "dp", flip)

    losses, query_total, own_part = local_call(
        functools.partial(own_grads_kernel, lists_of, scale),
        [((1, query_rows), f32), ((query_rows, width), f32), ((own_rows, width), f32)],
        hbm=(0,),
    )(
        table, scores_in, stats, far_stats, per_query, weights_own, queries, local, shares[0],
        *pieces,
    )
    (grad_queries,) = local_call(
        functools.partial(far_grads_kernel, lists_of, scale),
        [((query_rows, width), bf16)],
        scratch=[((query_rows, width), f32)],
        hbm=(0,),
    )(table, query_total, weights_far, *borrowed)
    collect = functools.partial(collect_kernel, shard_rows)
    last = returned.pop(1)
    (own_part,) = local_call(collect, [((own_rows, width), f32)])(own_part, *returned)
    (grad_passages,) = local_call(collect, [((own_rows, width), bf16)], hbm=(0,))(own_part, last)
    return (
        losses.reshape(query_rows),
        grad_queries,
        grad_passages.reshape(block_total, shard_rows, width),
    )


def per_device(queries, passages, block_lists, list_lengths, positive, loss_grad):
    plan = mirror_plan if mirror_fits(passages.shape) else exchange_plan
    return plan(queries, passages, block_lists, list_lengths, positive, loss_grad)


def solution(mesh):
    in_specs = (P("dp", "grp"), P(None, "dp", "grp"), P("dp", None), P("dp"), P("dp"), P("dp"))
    out_specs = (P("dp"), P("dp", "grp"), P(None, "dp", "grp"))
    return jax.shard_map(
        per_device, mesh=mesh, in_specs=in_specs, out_specs=out_specs, check_vma=False
    )
```
